32 devices in a mesh: groups: 2 (over x), seq: 16 (over z, y, core).
Axes of the slice: x: 2, y: 2, z: 4, core: 2. Of those that a mesh axis runs over, the one named last changes fastest.
Arguments:
- prefill_q: bfloat16 [32, 8192], P(('groups', 'seq')), parts along dimension 0, may hold values from -48 to 48
- cache_k: bfloat16 [16384, 1024], P(('groups', 'seq')), parts along dimension 0, may hold values from -4.5 to 4.5
- cache_v: bfloat16 [16384, 1024], P(('groups', 'seq')), parts along dimension 0, may hold values from -4.5 to 4.5
- page_counts: int32 [32], P('groups'), parts along dimension 0, may hold values from 1 to 64, 768 in all
- page_owner: int32 [2048, 1], P(('groups', 'seq')), parts along dimension 0, may hold values from 0 to 15; in each aligned block of 64 rows (0 to 63, 64 to 127, ...) at most 8 rows name the same one
- decode_q: bfloat16 [32, 2, 8192], P(('groups', 'seq')), parts along dimension 0, may hold values from -48 to 48
- decode_k: bfloat16 [32, 2, 1024], P(('groups', 'seq')), parts along dimension 0, may hold values from -12 to 12
- decode_v: bfloat16 [32, 2, 1024], P(('groups', 'seq')), parts along dimension 0, may hold values from -4.5 to 4.5
- context_len: int32 [32], P(('groups', 'seq')), parts along dimension 0, may hold values from 768 to 6144
Outputs:
- prefill_out: bfloat16 [32, 8192], P(('groups', 'seq')), parts along dimension 0
- decode_out: bfloat16 [32, 2, 8192], P(('groups', 'seq')), parts along dimension 0
- store_k: bfloat16 [32768, 1024], P(('groups', 'seq')), parts along dimension 0
- store_v: bfloat16 [32768, 1024], P(('groups', 'seq')), parts along dimension 0
- store_page: int32 [4096], P(('groups', 'seq')), parts along dimension 0
The draws below stay inside these ranges and needn't reach their ends.
There are 2 independent parts, one for each index of `groups`. The reference program is written for one: setup_inputs(seed, part) draws one part's arguments, and reference() takes and returns one part's arrays. A program takes and returns all parts, laid end to end along the dimension named above; each array names one. Nothing has to cross between parts.
Inputs may be any that keep to these rules, and one draw needn't show every extreme that they name: `page_counts`: the counts sum to 768 and the largest equals 64. `page_owner`: within the 64 page slots of one shard each owner is named at most 8 times, and exactly 8 times in some shards.
All inputs are finite; a program needn't handle non-finite values.
Results may differ from the reference program's by a relative error of at most 0.014.
Values may be sent and summed in bfloat16 or wider, within the bound.
No kernel may reach another device: no remote copies, remote signals or barrier semaphores. Data moves between devices by JAX's collectives and lax.ppermute only.
A program may use at most 128 MiB of HBM per device.

```python
import math
import jax
import jax.numpy as jnp
import numpy as np
from jax import lax

HQ = 64
KVH = 8
HD = 128
PAGE = 8
PPD = 64
STEPS = 2
KVD = 1024
CAP = 8
TOTAL_PAGES = 768
SLOTS = 1024
STORE = 2048
SPAN = 16
REQ = 16
N_SEQ = 16


def shared_keys(key):
    base_key = jax.random.fold_in(key, 11)
    key_table = jnp.clip(jax.random.normal(base_key, (SLOTS * PAGE, KVD), jnp.float32), -4.5, 4.5)
    return key_table


def shared_queries(key, height, salt_value):
    base_key = jax.random.fold_in(key, salt_value)
    drawn_rows = jnp.clip(2.5 * jax.random.normal(base_key, (height, HQ * HD), jnp.float32), -15.0, 15.0)
    final_rows = drawn_rows
    return (drawn_rows, final_rows)


def draw_prefill_q(key, part):
    return shared_queries(key, SPAN, 31)[1].astype(jnp.bfloat16)


def draw_cache_k(key, part):
    return shared_keys(key).astype(jnp.bfloat16)


def draw_decode_q(key, part):
    return shared_queries(key, REQ * STEPS, 41)[1].reshape(REQ, STEPS, HQ * HD).astype(jnp.bfloat16)


def draw_decode_k(key, part):
    drawn_rows = shared_queries(key, REQ * STEPS, 41)[0]
    grouping = HQ // KVH
    summed = jnp.sum(drawn_rows.reshape(REQ * STEPS, KVH, grouping, HD), axis=2) * (0.5 / jnp.sqrt(jnp.float32(grouping)))
    noise_part = 0.5 * jax.random.normal(jax.random.fold_in(key, 51), (REQ * STEPS, KVH, HD), jnp.float32)
    return jnp.clip(summed + noise_part, -12.0, 12.0).reshape(REQ, STEPS, KVH * HD).astype(jnp.bfloat16)


def with_ends(values, key, smallest, largest):
    longest = values.shape.index(max(values.shape))
    spots = []
    for shift in (0, 1):
        where = [jax.random.randint(jax.random.fold_in(key, axis), (), 0, length) for axis, length in enumerate(values.shape)]
        where[longest] = (where[longest] + shift) % values.shape[longest]
        spots.append(tuple(where))
    return values.at[spots[0]].set(smallest).at[spots[1]].set(largest)


def level_of(stream_key, shape, pieces, least, largest):
    gain, own = 1.0, jax.random.fold_in(stream_key, 6)
    for dim, shards_of in pieces:
        heights = jnp.exp(jax.random.uniform(jax.random.fold_in(own, dim), (shards_of,), jnp.float32, least / len(pieces), largest / len(pieces)))
        gain = gain * jnp.repeat(heights, shape[dim] // shards_of).reshape([-1 if axis == dim else 1 for axis in range(len(shape))])
    return gain


def length_profile(amount, total, most, skew):
    portions = [(1 << 20) // math.isqrt(grade ** skew) + 1 for grade in range(2, amount + 1)]
    spare, holding = total - most - (amount - 1), [1] * (amount - 1)
    while spare > 0:
        movable = [i for i in range(amount - 1) if holding[i] < most]
        pool, remaining = sum([portions[i] for i in movable]), spare
        for i in movable:
            extra = min(most - holding[i], max(1, remaining * portions[i] // pool), spare)
            holding[i] = holding[i] + extra
            spare = spare - extra
    return np.array([most] + holding)


def ragged_sizes(rng, number_of, total, most, skew):
    if number_of == 2:
        one = jax.random.randint(rng, (), max(1, total - most), min(most, total - 1) + 1)
        return jnp.stack([one, total - one])
    lengths = jnp.asarray(length_profile(number_of, total, most, skew), jnp.int32)
    pairs = (number_of - 1) // 2
    giver, taker = lengths[1:1 + 2 * pairs:2], lengths[2:2 + 2 * pairs:2]
    slack = jnp.minimum(giver - 1, most - taker)
    moved = jax.random.randint(jax.random.fold_in(rng, 1), (pairs,), 0, 1 << 20) % (slack + 1)
    lengths = lengths.at[1:1 + 2 * pairs:2].set(giver - moved).at[2:2 + 2 * pairs:2].set(taker + moved)
    return lengths[jax.random.permutation(jax.random.fold_in(rng, 2), number_of)]


def shared_out(own_key, own, number, rows, number_of, top, bound, lean):
    order = jax.random.permutation(own_key, number_of)
    packed, usual = load_shares(number_of, rows * top, bound, lean, True), load_shares(number_of, rows * top, bound, lean, False)
    places = jnp.arange(number_of)

    def named(tallies, rotation):
        used = int((tallies > 0).sum())
        fixed = max(1, used // 4)
        moved = fixed + (places - fixed + rotation * (used - fixed)) % max(1, number_of - fixed)
        return jnp.zeros((number_of,), jnp.int32).at[order[jnp.where(places < fixed, places, moved)]].set(jnp.asarray(tallies, jnp.int32))

    tallies = jnp.where(number % 4 == 0, named(packed, number // 4), named(usual, number - number // 4 - 1))
    mixed = jax.random.permutation(jax.random.fold_in(own, 3), number_of)
    source_of, taker = mixed[0:number_of // 2 * 2:2], mixed[1:number_of // 2 * 2:2]
    room = jnp.minimum(tallies[source_of] - 1, bound - tallies[taker]) // 2
    room = jnp.where((source_of == order[0]) | (taker == order[0]) | (tallies[taker] == 0), 0, jnp.maximum(room, 0))
    moved = jax.random.randint(jax.random.fold_in(own, 4), (number_of // 2,), 0, 1 << 20) % (room + 1)
    tallies = tallies.at[source_of].add(-moved).at[taker].add(moved)
    members = jnp.searchsorted(jnp.cumsum(tallies), jnp.arange(rows * top), side="right").astype(jnp.int32)
    table = members.reshape(top, rows).T
    table = table[jax.random.permutation(jax.random.fold_in(own, 1), rows)]
    rotation = jax.random.randint(jax.random.fold_in(own, 2), (rows, 1), 0, top)
    return jnp.take_along_axis(table, (jnp.arange(top)[None, :] + rotation) % top, axis=1)


def load_shares(number_of, total, most, slope, full):
    portions = [(1 << 20) // math.isqrt(standing ** slope) + 1 for standing in range(1, number_of + 1)]
    largest = most if full else min(most, max(-(-total // number_of), total * portions[0] // sum(portions)))
    least = 1 if total - largest >= number_of - 1 else 0
    given, rest = [largest] + [least] * (number_of - 1), total - largest - least * (number_of - 1)
    while rest > 0:
        candidates = [i for i in range(1, number_of) if given[i] < largest] or [i for i in range(1, number_of) if given[i] < most]
        mass, left = sum([portions[i] for i in candidates]), rest
        for i in candidates:
            addition = min(most - given[i], max(1, left * portions[i] // mass), rest)
            given[i] = given[i] + addition
            rest = rest - addition
    return np.array(given)


def bell_draw(own_key, dims, spread, limit, shards=(), held_as=jnp.bfloat16):
    drawn = spread * jax.random.normal(own_key, dims, jnp.float32)
    if shards:
        drawn = drawn * level_of(own_key, dims, shards, -0.22, 0.18)
    return jnp.clip(drawn, -limit, limit).astype(held_as)


def setup_inputs(seed: int = 0, part: int = 0) -> dict:
    splits = jax.random.split(jax.random.key(seed), 10)
    part_keys = jax.random.split(jax.random.fold_in(splits[9], part), 10)
    prefill_q = draw_prefill_q(jax.random.fold_in(jax.random.fold_in(splits[9], part), 71), part)
    cache_k = draw_cache_k(jax.random.fold_in(jax.random.fold_in(splits[9], part), 71), part)
    cache_v = bell_draw(part_keys[2], (SLOTS * PAGE, KVD), 1.0, 4.5, ((0, 16),))
    page_counts = ragged_sizes(part_keys[3], N_SEQ, TOTAL_PAGES, PPD, 2).astype(jnp.int32)
    page_owner_keys = jax.random.split(jax.random.fold_in(part_keys[4], 1), SLOTS // PPD)
    page_owner_turns = jax.random.permutation(jax.random.fold_in(part_keys[4], 3), SLOTS // PPD)
    page_owner = jax.vmap(lambda own, number: shared_out(jax.random.fold_in(part_keys[4], 2), own, number, PPD, N_SEQ, 1, CAP, 2))(page_owner_keys, page_owner_turns).reshape((SLOTS, 1))
    decode_q = draw_decode_q(jax.random.fold_in(jax.random.fold_in(splits[9], part), 71), part)
    decode_k = draw_decode_k(jax.random.fold_in(jax.random.fold_in(splits[9], part), 71), part)
    decode_v = bell_draw(part_keys[7], (REQ, STEPS, KVD), 1.0, 4.5, ((0, 16),))
    context_len = with_ends(jax.random.randint(part_keys[8], (REQ,), PAGE * TOTAL_PAGES // 8, PAGE * TOTAL_PAGES + 1), jax.random.fold_in(part_keys[8], 1), PAGE * TOTAL_PAGES // 8, PAGE * TOTAL_PAGES).astype(jnp.int32)
    return dict(prefill_q=prefill_q, cache_k=cache_k, cache_v=cache_v, page_counts=page_counts, page_owner=page_owner, decode_q=decode_q, decode_k=decode_k, decode_v=decode_v, context_len=context_len)


MASKED = -1.0e30
EXACT = lax.Precision.HIGHEST


def attention(queries, key_block, value_block, allowed, own_keys, own_values, own_allowed):
    height = queries.shape[0]
    grouping = HQ // KVH
    scaling = HD ** -0.5
    query_all = queries.astype(jnp.float32).reshape(height, KVH, grouping, HD)
    key_all = key_block.astype(jnp.float32).reshape(-1, KVH, HD)
    value_all = value_block.astype(jnp.float32).reshape(-1, KVH, HD)
    if own_keys is not None:
        own_key_all = own_keys.astype(jnp.float32).reshape(height, -1, KVH, HD)
        own_value_all = own_values.astype(jnp.float32).reshape(height, -1, KVH, HD)

    def per_group(member):
        query_group = lax.dynamic_index_in_dim(query_all, member, 1, keepdims=False)
        key_group = lax.dynamic_index_in_dim(key_all, member, 1, keepdims=False)
        value_group = lax.dynamic_index_in_dim(value_all, member, 1, keepdims=False)
        scores = jnp.einsum("qhd,kd->qhk", query_group, key_group, precision=EXACT) * scaling
        scores = jnp.where(allowed[:, None, :], scores, MASKED)
        highest = jnp.max(scores, axis=2)
        if own_keys is not None:
            own_key_group = lax.dynamic_index_in_dim(own_key_all, member, 2, keepdims=False)
            own_value_group = lax.dynamic_index_in_dim(own_value_all, member, 2, keepdims=False)
            own_scores = jnp.einsum("qhd,qtd->qht", query_group, own_key_group, precision=EXACT) * scaling
            own_scores = jnp.where(own_allowed[:, None, :], own_scores, MASKED)
            highest = jnp.maximum(highest, jnp.max(own_scores, axis=2))
        weights = jnp.where(allowed[:, None, :], jnp.exp(scores - highest[:, :, None]), 0.0)
        totals = jnp.sum(weights, axis=2)
        if own_keys is not None:
            own_weights = jnp.where(own_allowed[:, None, :], jnp.exp(own_scores - highest[:, :, None]), 0.0)
            totals = totals + jnp.sum(own_weights, axis=2)
        probs = lax.optimization_barrier((weights / totals[:, :, None]).astype(jnp.bfloat16)).astype(jnp.float32)
        result = jnp.einsum("qhk,kd->qhd", probs, value_group, precision=EXACT)
        if own_keys is not None:
            own_probs = lax.optimization_barrier((own_weights / totals[:, :, None]).astype(jnp.bfloat16)).astype(jnp.float32)
            result = result + jnp.einsum("qht,qtd->qhd", own_probs, own_value_group, precision=EXACT)
        return result

    outputs = lax.map(per_group, jnp.arange(KVH, dtype=jnp.int32))
    return outputs.transpose(1, 0, 2, 3).reshape(height, HQ * HD).astype(jnp.bfloat16)


def reference(prefill_q, cache_k, cache_v, page_counts, page_owner, decode_q, decode_k, decode_v, context_len):
    shard_rows = PPD * PAGE
    key_rows = jnp.arange(SLOTS * PAGE, dtype=jnp.int32)
    device_of = key_rows // shard_rows
    local_row = key_rows % shard_rows
    before = (jnp.cumsum(page_counts) - page_counts).astype(jnp.int32)
    usable = local_row < PAGE * page_counts[device_of]
    places = PAGE * before[device_of] + local_row
    prompt = PAGE * jnp.sum(page_counts).astype(jnp.int32)
    query_places = prompt - SPAN + jnp.arange(SPAN, dtype=jnp.int32)
    allowed = usable[None, :] & (places[None, :] <= query_places[:, None])
    prefill_out = attention(prefill_q, cache_k, cache_v, allowed, None, None, None)

    query_rows = decode_q.reshape(REQ * STEPS, HQ * HD)
    limits = jnp.repeat(context_len, STEPS)
    decode_allowed = usable[None, :] & (places[None, :] < limits[:, None])
    own_keys = jnp.repeat(decode_k, STEPS, axis=0)
    own_values = jnp.repeat(decode_v, STEPS, axis=0)
    steps_now = jnp.tile(jnp.arange(STEPS, dtype=jnp.int32), REQ)
    own_allowed = jnp.arange(STEPS, dtype=jnp.int32)[None, :] <= steps_now[:, None]
    decode_out = attention(query_rows, cache_k, cache_v, decode_allowed, own_keys, own_values, own_allowed)
    decode_out = decode_out.reshape(REQ, STEPS, HQ * HD)

    owners = page_owner[:, 0]
    page_index = jnp.arange(SLOTS, dtype=jnp.int32)
    page_device = page_index // PPD
    page_live = (page_index % PPD) < page_counts[page_device]
    chosen = owners[:, None] == jnp.arange(N_SEQ, dtype=jnp.int32)[None, :]
    chosen_live = (chosen & page_live[:, None]).astype(jnp.int32).reshape(N_SEQ, PPD, N_SEQ)
    earlier = (jnp.cumsum(chosen_live, axis=1) - chosen_live).astype(jnp.int32).reshape(SLOTS, N_SEQ)
    ranking = jnp.sum(earlier * chosen.astype(jnp.int32), axis=1).astype(jnp.int32)
    target = jnp.where(page_live, owners * (N_SEQ * CAP) + page_device * CAP + ranking, STORE).astype(jnp.int32)
    store_k = jnp.zeros((STORE, PAGE * KVD), cache_k.dtype).at[target].set(cache_k.reshape(SLOTS, PAGE * KVD), mode="drop")
    store_v = jnp.zeros((STORE, PAGE * KVD), cache_v.dtype).at[target].set(cache_v.reshape(SLOTS, PAGE * KVD), mode="drop")
    store_page = jnp.full((STORE,), -1, jnp.int32).at[target].set(page_index, mode="drop")
    return prefill_out, decode_out, store_k.reshape(STORE * PAGE, KVD), store_v.reshape(STORE * PAGE, KVD), store_page
```

```python
import functools
import jax
import jax.numpy as jnp
from jax import lax
from jax.experimental import pallas as pl
from jax.experimental.pallas import tpu as pltpu
from jax.sharding import PartitionSpec as P

HQ = 64
KVH = 8
HD = 128
PAGE = 8
STEPS = 2
KVD = 1024
GRP = HQ // KVH
MASKED = -1e30
VMEM = pltpu.MemorySpace.VMEM
SMEM = pltpu.MemorySpace.SMEM
LIMIT = 48 * 1024 * 1024


def whole(space):
    return pl.BlockSpec(memory_space=space)


def message_kernel(rows_p, rows_d, length, prefill_q, decode_q, owners, out, rows):
    for r in range(rows_p + rows_d):
        ref, at = (prefill_q, r) if r < rows_p else (decode_q, r - rows_p)
        line = ref[at : at + 1, :].astype(jnp.float32)
        for h in range(HQ):
            rows[r * HQ + h : r * HQ + h + 1, :] = line[:, h * HD : (h + 1) * HD]
    base = (rows_p + rows_d) * HQ
    slots = owners.shape[1]
    rows[base : base + 8, :] = jnp.zeros((8, 128), jnp.float32)
    rows[base : base + 1, 0:slots] = owners[...].astype(jnp.float32)
    lane = lax.broadcasted_iota(jnp.int32, (1, 128), 1)
    digits = jnp.zeros((1, 128), jnp.int32)
    for q in range(length.shape[0]):
        value = length[q]
        digits = jnp.where(lane == 2 * q, value // 256, digits)
        digits = jnp.where(lane == 2 * q + 1, value % 256, digits)
    rows[base + 1 : base + 2, :] = digits.astype(jnp.float32)
    out[...] = rows[...].reshape(out.shape).astype(jnp.bfloat16)


def make_message(prefill_q, decode_q, page_owner, context_len):
    rows_p = prefill_q.shape[0]
    rows_d = decode_q.shape[0] * STEPS
    blocks = (rows_p + rows_d) * KVH + 1
    return pl.pallas_call(
        functools.partial(message_kernel, rows_p, rows_d),
        out_shape=jax.ShapeDtypeStruct((blocks, 8, 128), jnp.bfloat16),
        in_specs=[whole(SMEM), whole(VMEM), whole(VMEM), whole(VMEM)],
        out_specs=whole(VMEM),
        scratch_shapes=[pltpu.VMEM((blocks * 8, 128), jnp.float32)],
        name="message",
    )(context_len, prefill_q, decode_q.reshape(rows_d, HQ * HD), page_owner.reshape(1, -1))


def pack_kernel(shards, capacity, owners, counts, pages, out, held, blank, taken, sem_in, sem_out):
    me = lax.axis_index("seq")
    fetch = pltpu.make_async_copy(pages, held, sem_in)
    fetch.start()
    blank[...] = jnp.zeros_like(blank)

    def reset(o, carry):
        taken[o] = 0
        return carry

    lax.fori_loop(0, shards, reset, 0)
    fetch.wait()

    def place(j, carry):
        o = owners[j]
        k = taken[o]
        taken[o] = k + 1
        pltpu.make_async_copy(held.at[j], out.at[o * capacity + k], sem_out).start()
        return carry

    lax.fori_loop(0, counts[me], place, 0)

    def fill(o, carry):
        def one(k, inner):
            pltpu.make_async_copy(blank, out.at[o * capacity + k], sem_out).start()
            return inner

        return lax.fori_loop(taken[o], capacity, one, carry)

    lax.fori_loop(0, shards, fill, 0)
    pltpu.make_async_copy(out, out, sem_out).wait()


def pack(owners, counts, pages, shards, capacity):
    slots = pages.shape[0]
    return pl.pallas_call(
        functools.partial(pack_kernel, shards, capacity),
        out_shape=jax.ShapeDtypeStruct((shards * capacity, PAGE, KVD), pages.dtype),
        in_specs=[whole(SMEM), whole(SMEM), whole(pl.ANY)],
        out_specs=whole(pl.ANY),
        scratch_shapes=[
            pltpu.VMEM((slots, PAGE, KVD), pages.dtype),
            pltpu.VMEM((PAGE, KVD), pages.dtype),
            pltpu.SMEM((shards,), jnp.int32),
            pltpu.SemaphoreType.DMA,
            pltpu.SemaphoreType.DMA,
        ],
        cost_estimate=pl.CostEstimate(
            flops=0, transcendentals=0, bytes_accessed=(slots + shards * capacity) * PAGE * KVD * 2
        ),
        name="pack",
    )(owners, counts, pages)


def attend_kernel(
    rows_p, rows_d, capacity, counts, message, keys, values, out, table, limits, stats, hits
):
    me = lax.axis_index("seq")
    shards = message.shape[0]
    rows = rows_p + rows_d
    height = shards * rows * GRP
    held = keys.shape[0]

    def count(d, carry):
        before, total = carry
        here = counts[d]
        return (before + jnp.where(d < me, here, 0), total + here)

    before, total = lax.fori_loop(0, shards, count, (jnp.int32(0), jnp.int32(0)))
    start = PAGE * before
    live = PAGE * counts[me]
    first = PAGE * total - shards * rows_p + 1
    lane = lax.broadcasted_iota(jnp.int32, (1, 128), 1)
    last = rows * KVH
    for d in range(shards):
        tail = message[d, last].astype(jnp.float32)
        for r in range(rows):
            at = (d * rows + r) * GRP
            if r < rows_p:
                bound = jnp.minimum(first + d * rows_p + r - start, live)
                limits[at : at + GRP, :] = jnp.full((GRP, 128), bound, jnp.int32)
            else:
                q = (r - rows_p) // STEPS
                length = tail[1:2, 2 * q : 2 * q + 1] * 256.0 + tail[1:2, 2 * q + 1 : 2 * q + 2]
                bound = jnp.minimum(length.astype(jnp.int32) - start, live)
                limits[at : at + GRP, :] = jnp.broadcast_to(bound, (GRP, 128))
        hit = (tail[0:1, :].astype(jnp.int32) == me) & (lane < counts[d])
        hits[d : d + 1, :] = hit.astype(jnp.float32)

    hit = hits[...]
    earlier = (
        lax.broadcasted_iota(jnp.int32, (128, 128), 0)
        < lax.broadcasted_iota(jnp.int32, (128, 128), 1)
    ).astype(jnp.bfloat16)
    rank = jnp.dot(hit.astype(jnp.bfloat16), earlier, preferred_element_type=jnp.float32)
    wide = lax.broadcasted_iota(jnp.int32, hit.shape, 1)
    depth = lax.broadcasted_iota(jnp.int32, hit.shape, 0)
    numbered = jnp.zeros(hit.shape, jnp.float32)
    for k in range(capacity):
        match = jnp.where((hit > 0.5) & (rank == float(k)), (wide + 1).astype(jnp.float32), 0.0)
        found = jnp.sum(match, axis=1, keepdims=True)
        numbered = jnp.where(wide == k, found, numbered)
    within = numbered.astype(jnp.int32)
    slots = held // PAGE
    table[...] = jnp.where(within > 0, depth * slots + within - 1, -1)

    stats[...] = jnp.zeros_like(stats)
    spot = lax.broadcasted_iota(jnp.int32, (height, 128), 1)
    column = lax.broadcasted_iota(jnp.int32, (height, held), 1)

    def one_group(g, carry):
        query = jnp.concatenate(
            [
                message[d, r * KVH + g].astype(jnp.float32)
                for d in range(shards)
                for r in range(rows)
            ],
            axis=0,
        ).astype(jnp.bfloat16)
        across = pl.ds(pl.multiple_of(g * HD, HD), HD)
        scores = lax.dot_general(
            query, keys[:, across], (((1,), (1,)), ((), ())), preferred_element_type=jnp.float32
        ) * (HD ** (-0.5))
        allowed = column < jnp.concatenate([limits[...]] * (held // 128), axis=1)
        scores = jnp.where(allowed, scores, MASKED)
        high = jnp.max(scores, axis=1, keepdims=True).astype(jnp.bfloat16).astype(jnp.float32)
        weights = jnp.where(allowed, jnp.exp(scores - high), 0.0)
        total = jnp.sum(weights, axis=1, keepdims=True)
        product = jnp.dot(
            weights.astype(jnp.bfloat16), values[:, across], preferred_element_type=jnp.float32
        )
        coarse = total.astype(jnp.bfloat16).astype(jnp.float32)
        kept = jnp.where(spot == g, high, stats[...])
        kept = jnp.where(spot == KVH + g, coarse, kept)
        stats[...] = jnp.where(spot == 2 * KVH + g, total - coarse, kept)
        for d in range(shards):
            for r in range(rows):
                at = (d * rows + r) * GRP
                out[d, r * KVH + g] = product[at : at + GRP, :].astype(jnp.bfloat16)
        return carry

    lax.fori_loop(0, KVH, one_group, 0)
    for d in range(shards):
        for r in range(rows):
            at = (d * rows + r) * GRP
            out[d, rows * KVH + r] = stats[at : at + GRP, :].astype(jnp.bfloat16)


def attend(rows_p, rows_d, capacity, counts, message, keys, values):
    shards = message.shape[0]
    rows = rows_p + rows_d
    height = shards * rows * GRP
    held = keys.shape[0]
    return pl.pallas_call(
        functools.partial(attend_kernel, rows_p, rows_d, capacity),
        out_shape=(
            jax.ShapeDtypeStruct((shards, rows * (KVH + 1), GRP, 128), jnp.bfloat16),
            jax.ShapeDtypeStruct((shards, 128), jnp.int32),
        ),
        in_specs=[whole(SMEM), whole(VMEM), whole(VMEM), whole(VMEM)],
        out_specs=(whole(VMEM), whole(VMEM)),
        scratch_shapes=[
            pltpu.VMEM((height, 128), jnp.int32),
            pltpu.VMEM((height, 128), jnp.float32),
            pltpu.VMEM((shards, 128), jnp.float32),
        ],
        compiler_params=pltpu.CompilerParams(vmem_limit_bytes=LIMIT),
        cost_estimate=pl.CostEstimate(
            flops=4 * height * KVH * held * HD,
            transcendentals=height * KVH * held,
            bytes_accessed=2 * held * KVD * 2 + 4 * height * KVH * HD,
        ),
        name="attend",
    )(counts, message, keys, values)


def merge_kernel(rows_p, rows_d, parts, message, new_k, new_v, prefill_out, decode_out, lines):
    sources = parts.shape[0]
    rows = rows_p + rows_d
    lane = lax.broadcasted_iota(jnp.int32, (GRP, 128), 1)
    for r in range(rows):
        raw = [parts[s, rows * KVH + r].astype(jnp.float32) for s in range(sources)]
        high = functools.reduce(jnp.maximum, raw)
        fresh = []
        if r >= rows_p:
            request, step = divmod(r - rows_p, STEPS)
            for t in range(step + 1):
                score = jnp.zeros((GRP, 128), jnp.float32)
                for g in range(KVH):
                    query = message[r * KVH + g].astype(jnp.float32)
                    at = request * STEPS + t
                    key = new_k[at : at + 1, g * HD : (g + 1) * HD].astype(jnp.float32)
                    column = jnp.sum(query * key, axis=1, keepdims=True) * (HD ** (-0.5))
                    score = jnp.where(lane == g, column, score)
                fresh.append((request * STEPS + t, score))
                high = jnp.maximum(high, score)
        high = jnp.where(lane < KVH, high, 0.0)
        total = jnp.zeros((GRP, 128), jnp.float32)
        factors = []
        for s in range(sources):
            factor = jnp.exp(jnp.where(lane < KVH, raw[s], 0.0) - high)
            size = pltpu.roll(raw[s], 128 - KVH, 1) + pltpu.roll(raw[s], 128 - 2 * KVH, 1)
            total = total + factor * size
            factors.append(factor)
        fresh = [(at, jnp.exp(score - high)) for at, score in fresh]
        for _, weight in fresh:
            total = total + weight
        total = jnp.where(lane < KVH, total, 1.0)
        factors = [factor / total for factor in factors]
        fresh = [
            (at, (weight / total).astype(jnp.bfloat16).astype(jnp.float32)) for at, weight in fresh
        ]
        for g in range(KVH):
            result = jnp.zeros((GRP, HD), jnp.float32)
            for s in range(sources):
                result = result + factors[s][:, g : g + 1] * parts[s, r * KVH + g].astype(jnp.float32)
            for at, weight in fresh:
                value = new_v[at : at + 1, g * HD : (g + 1) * HD].astype(jnp.float32)
                result = result + weight[:, g : g + 1] * value
            for h in range(GRP):
                column = (g * GRP + h) * HD
                lines[r : r + 1, column : column + HD] = result[h : h + 1, :]
    prefill_out[...] = lines[0:rows_p, :].astype(jnp.bfloat16)
    decode_out[...] = lines[rows_p:rows, :].astype(jnp.bfloat16)


def merge(rows_p, rows_d, parts, message, new_k, new_v):
    rows = rows_p + rows_d
    return pl.pallas_call(
        functools.partial(merge_kernel, rows_p, rows_d),
        out_shape=(
            jax.ShapeDtypeStruct((rows_p, HQ * HD), jnp.bfloat16),
            jax.ShapeDtypeStruct((rows_d, HQ * HD), jnp.bfloat16),
        ),
        in_specs=[whole(VMEM)] * 4,
        out_specs=(whole(VMEM), whole(VMEM)),
        scratch_shapes=[pltpu.VMEM((rows, HQ * HD), jnp.float32)],
        compiler_params=pltpu.CompilerParams(vmem_limit_bytes=LIMIT),
        cost_estimate=pl.CostEstimate(
            flops=parts.size * 4, transcendentals=0, bytes_accessed=parts.size * 2
        ),
        name="merge",
    )(parts, message, new_k.reshape(rows_d, KVD), new_v.reshape(rows_d, KVD))


def exchange(array):
    return lax.all_to_all(array, "seq", split_axis=0, concat_axis=0, tiled=True)


def per_device(
    prefill_q, cache_k, cache_v, page_counts, page_owner, decode_q, decode_k, decode_v, context_len
):
    shards = lax.axis_size("seq")
    page_slots = cache_k.shape[0] // PAGE
    capacity = max(2, 2 * page_slots // shards)
    rows_p = prefill_q.shape[0]
    rows_d = decode_q.shape[0] * STEPS
    owners = page_owner.reshape(-1)
    pages_k = cache_k.reshape(page_slots, PAGE, KVD)
    pages_v = cache_v.reshape(page_slots, PAGE, KVD)
    message = make_message(prefill_q, decode_q, page_owner, context_len)
    gathered = lax.all_gather(message, "seq", axis=0)
    packed_k = pack(owners, page_counts, pages_k, shards, capacity)
    packed_v = pack(owners, page_counts, pages_v, shards, capacity)
    packed_k, gathered = lax.optimization_barrier((packed_k, gathered))
    store_k = exchange(packed_k)
    parts, table = attend(rows_p, rows_d, capacity, page_counts, gathered, cache_k, cache_v)
    packed_v, parts, store_k = lax.optimization_barrier((packed_v, parts, store_k))
    received = exchange(parts)
    packed_v, received = lax.optimization_barrier((packed_v, received))
    store_v = exchange(packed_v)
    prefill_out, decode_out = merge(
        rows_p, rows_d, received, message, decode_k, decode_v
    )
    store_page = table[:, :capacity].reshape(-1)
    return (
        prefill_out,
        decode_out.reshape(decode_q.shape),
        store_k.reshape(-1, KVD),
        store_v.reshape(-1, KVD),
        store_page,
    )


def solution(mesh):
    in_specs = (
        P(("groups", "seq"), None),
        P(("groups", "seq"), None),
        P(("groups", "seq"), None),
        P("groups"),
        P(("groups", "seq"), None),
        P(("groups", "seq"), None, None),
        P(("groups", "seq"), None, None),
        P(("groups", "seq"), None, None),
        P(("groups", "seq")),
    )
    out_specs = (
        P(("groups", "seq"), None),
        P(("groups", "seq"), None, None),
        P(("groups", "seq"), None),
        P(("groups", "seq"), None),
        P(("groups", "seq")),
    )
    return jax.shard_map(
        per_device, mesh=mesh, in_specs=in_specs, out_specs=out_specs, check_vma=False
    )
```

```python
import functools
import jax
import jax.numpy as jnp
from jax import lax
from jax.experimental import pallas as pl
from jax.experimental.pallas import tpu as pltpu
from jax.sharding import PartitionSpec as P

HQ = 64
KVH = 8
HD = 128
PAGE = 8
STEPS = 2
KVD = 1024
GRP = HQ // KVH
MASKED = -1e30
VMEM = pltpu.MemorySpace.VMEM
SMEM = pltpu.MemorySpace.SMEM
LIMIT = 48 * 1024 * 1024


def whole(space):
    return pl.BlockSpec(memory_space=space)


def message_kernel(rows_p, rows_d, length, prefill_q, decode_q, owners, out, rows):
    for r in range(rows_p + rows_d):
        ref, at = (prefill_q, r) if r < rows_p else (decode_q, r - rows_p)
        line = ref[at : at + 1, :].astype(jnp.float32)
        for h in range(HQ):
            rows[r * HQ + h : r * HQ + h + 1, :] = line[:, h * HD : (h + 1) * HD]
    base = (rows_p + rows_d) * HQ
    slots = owners.shape[1]
    rows[base : base + 8, :] = jnp.zeros((8, 128), jnp.float32)
    rows[base : base + 1, 0:slots] = owners[...].astype(jnp.float32)
    lane = lax.broadcasted_iota(jnp.int32, (1, 128), 1)
    digits = jnp.zeros((1, 128), jnp.int32)
    for q in range(length.shape[0]):
        value = length[q]
        digits = jnp.where(lane == 2 * q, value // 256, digits)
        digits = jnp.where(lane == 2 * q + 1, value % 256, digits)
    rows[base + 1 : base + 2, :] = digits.astype(jnp.float32)
    out[...] = rows[...].reshape(out.shape).astype(jnp.bfloat16)


def make_message(prefill_q, decode_q, page_owner, context_len):
    rows_p = prefill_q.shape[0]
    rows_d = decode_q.shape[0] * STEPS
    blocks = (rows_p + rows_d) * KVH + 1
    return pl.pallas_call(
        functools.partial(message_kernel, rows_p, rows_d),
        out_shape=jax.ShapeDtypeStruct((blocks, 8, 128), jnp.bfloat16),
        in_specs=[whole(SMEM), whole(VMEM), whole(VMEM), whole(VMEM)],
        out_specs=whole(VMEM),
        scratch_shapes=[pltpu.VMEM((blocks * 8, 128), jnp.float32)],
        name="message",
    )(context_len, prefill_q, decode_q.reshape(rows_d, HQ * HD), page_owner.reshape(1, -1))


def pack_kernel(shards, capacity, owners, counts, pages, out, held, blank, taken, sem_in, sem_out):
    me = lax.axis_index("seq")
    fetch = pltpu.make_async_copy(pages, held, sem_in)
    fetch.start()
    blank[...] = jnp.zeros_like(blank)

    def reset(o, carry):
        taken[o] = 0
        return carry

    lax.fori_loop(0, shards, reset, 0)
    fetch.wait()

    def place(j, carry):
        o = owners[j]
        k = taken[o]
        taken[o] = k + 1
        pltpu.make_async_copy(held.at[j], out.at[o * capacity + k], sem_out).start()
        return carry

    lax.fori_loop(0, counts[me], place, 0)

    def fill(o, carry):
        def one(k, inner):
            pltpu.make_async_copy(blank, out.at[o * capacity + k], sem_out).start()
            return inner

        return lax.fori_loop(taken[o], capacity, one, carry)

    lax.fori_loop(0, shards, fill, 0)
    pltpu.make_async_copy(out, out, sem_out).wait()


def pack(owners, counts, pages, shards, capacity):
    slots = pages.shape[0]
    return pl.pallas_call(
        functools.partial(pack_kernel, shards, capacity),
        out_shape=jax.ShapeDtypeStruct((shards * capacity, PAGE, KVD), pages.dtype),
        in_specs=[whole(SMEM), whole(SMEM), whole(pl.ANY)],
        out_specs=whole(pl.ANY),
        scratch_shapes=[
            pltpu.VMEM((slots, PAGE, KVD), pages.dtype),
            pltpu.VMEM((PAGE, KVD), pages.dtype),
            pltpu.SMEM((shards,), jnp.int32),
            pltpu.SemaphoreType.DMA,
            pltpu.SemaphoreType.DMA,
        ],
        cost_estimate=pl.CostEstimate(
            flops=0, transcendentals=0, bytes_accessed=(slots + shards * capacity) * PAGE * KVD * 2
        ),
        name="pack",
    )(owners, counts, pages)


def attend_kernel(rows_p, rows_d, capacity, counts, *refs):
    messages, refs = refs[:4], refs[4:]
    keys, values, keep, give, table, limits, stats, hits = refs
    me = lax.axis_index("seq")
    rows = rows_p + rows_d
    blocks = rows * KVH + 1
    shards = 4 * messages[0].shape[0] // blocks
    height = shards * rows * GRP
    held = keys.shape[0]

    def block(k, at):
        return messages[k % 4][(k // 4) * blocks + at]

    def count(d, carry):
        before, total = carry
        here = counts[d]
        return (before + jnp.where(d < me, here, 0), total + here)

    before, total = lax.fori_loop(0, shards, count, (jnp.int32(0), jnp.int32(0)))
    start = PAGE * before
    live = PAGE * counts[me]
    first = PAGE * total - shards * rows_p + 1
    lane = lax.broadcasted_iota(jnp.int32, (1, 128), 1)
    for k in range(shards):
        d = me ^ k
        tail = block(k, rows * KVH).astype(jnp.float32)
        for r in range(rows):
            at = (k * rows + r) * GRP
            if r < rows_p:
                bound = jnp.minimum(first + d * rows_p + r - start, live)
                limits[at : at + GRP, :] = jnp.full((GRP, 128), bound, jnp.int32)
            else:
                q = (r - rows_p) // STEPS
                length = tail[1:2, 2 * q : 2 * q + 1] * 256.0 + tail[1:2, 2 * q + 1 : 2 * q + 2]
                bound = jnp.minimum(length.astype(jnp.int32) - start, live)
                limits[at : at + GRP, :] = jnp.broadcast_to(bound, (GRP, 128))
        hit = (tail[0:1, :].astype(jnp.int32) == me) & (lane < counts[d])
        hits[pl.ds(d, 1), :] = hit.astype(jnp.float32)

    hit = hits[...]
    earlier = (
        lax.broadcasted_iota(jnp.int32, (128, 128), 0)
        < lax.broadcasted_iota(jnp.int32, (128, 128), 1)
    ).astype(jnp.bfloat16)
    rank = jnp.dot(hit.astype(jnp.bfloat16), earlier, preferred_element_type=jnp.float32)
    wide = lax.broadcasted_iota(jnp.int32, hit.shape, 1)
    depth = lax.broadcasted_iota(jnp.int32, hit.shape, 0)
    numbered = jnp.zeros(hit.shape, jnp.float32)
    for k in range(capacity):
        match = jnp.where((hit > 0.5) & (rank == float(k)), (wide + 1).astype(jnp.float32), 0.0)
        found = jnp.sum(match, axis=1, keepdims=True)
        numbered = jnp.where(wide == k, found, numbered)
    within = numbered.astype(jnp.int32)
    slots = held // PAGE
    table[...] = jnp.where(within > 0, depth * slots + within - 1, -1)

    stats[...] = jnp.zeros_like(stats)
    spot = lax.broadcasted_iota(jnp.int32, (height, 128), 1)
    column = lax.broadcasted_iota(jnp.int32, (height, held), 1)
    pieces = [(k, r, (k * rows + r) * GRP) for k in range(shards) for r in range(rows)]

    def target(k):
        return give if k % 2 else keep

    def one_group(g, carry):
        query = jnp.concatenate(
            [block(k, r * KVH + g).astype(jnp.float32) for k, r, _ in pieces], axis=0
        ).astype(jnp.bfloat16)
        across = pl.ds(pl.multiple_of(g * HD, HD), HD)
        scores = lax.dot_general(
            query, keys[:, across], (((1,), (1,)), ((), ())), preferred_element_type=jnp.float32
        ) * (HD ** (-0.5))
        allowed = column < jnp.concatenate([limits[...]] * (held // 128), axis=1)
        scores = jnp.where(allowed, scores, MASKED)
        high = jnp.max(scores, axis=1, keepdims=True).astype(jnp.bfloat16).astype(jnp.float32)
        weights = jnp.where(allowed, jnp.exp(scores - high), 0.0)
        total = jnp.sum(weights, axis=1, keepdims=True)
        product = jnp.dot(
            weights.astype(jnp.bfloat16), values[:, across], preferred_element_type=jnp.float32
        )
        coarse = total.astype(jnp.bfloat16).astype(jnp.float32)
        kept = jnp.where(spot == g, high, stats[...])
        kept = jnp.where(spot == KVH + g, coarse, kept)
        stats[...] = jnp.where(spot == 2 * KVH + g, total - coarse, kept)
        for k, r, at in pieces:
            target(k)[k // 2, r * KVH + g] = product[at : at + GRP, :].astype(jnp.bfloat16)
        return carry

    lax.fori_loop(0, KVH, one_group, 0)
    for k, r, at in pieces:
        target(k)[k // 2, rows * KVH + r] = stats[at : at + GRP, :].astype(jnp.bfloat16)


def attend(rows_p, rows_d, capacity, counts, messages, keys, values):
    rows = rows_p + rows_d
    shards = 4 * messages[0].shape[0] // (rows * KVH + 1)
    height = shards * rows * GRP
    held = keys.shape[0]
    half = jax.ShapeDtypeStruct((shards // 2, rows * (KVH + 1), GRP, 128), jnp.bfloat16)
    return pl.pallas_call(
        functools.partial(attend_kernel, rows_p, rows_d, capacity),
        out_shape=(half, half, jax.ShapeDtypeStruct((shards, 128), jnp.int32)),
        in_specs=[whole(SMEM)] + [whole(VMEM)] * 6,
        out_specs=(whole(VMEM),) * 3,
        scratch_shapes=[
            pltpu.VMEM((height, 128), jnp.int32),
            pltpu.VMEM((height, 128), jnp.float32),
            pltpu.VMEM((shards, 128), jnp.float32),
        ],
        compiler_params=pltpu.CompilerParams(vmem_limit_bytes=LIMIT),
        cost_estimate=pl.CostEstimate(
            flops=4 * height * KVH * held * HD,
            transcendentals=height * KVH * held,
            bytes_accessed=2 * held * KVD * 2 + 4 * height * KVH * HD,
        ),
        name="attend",
    )(counts, *messages, keys, values)


def fold_kernel(rows, keep, got, *outs):
    lane = lax.broadcasted_iota(jnp.int32, (GRP, 128), 1)
    inside = lane < KVH
    for j, out in enumerate(outs):
        for r in range(rows):
            raw = [ref[j, rows * KVH + r].astype(jnp.float32) for ref in (keep, got)]
            high = jnp.maximum(jnp.where(inside, raw[0], 0.0), jnp.where(inside, raw[1], 0.0))
            factors = [jnp.exp(jnp.where(inside, part, 0.0) - high) for part in raw]
            sizes = [
                pltpu.roll(part, 128 - KVH, 1) + pltpu.roll(part, 128 - 2 * KVH, 1) for part in raw
            ]
            total = jnp.where(inside, factors[0] * sizes[0] + factors[1] * sizes[1], 0.0)
            coarse = total.astype(jnp.bfloat16).astype(jnp.float32)
            line = high + pltpu.roll(coarse, KVH, 1) + pltpu.roll(total - coarse, 2 * KVH, 1)
            out[rows * KVH + r] = line.astype(jnp.bfloat16)
            for g in range(KVH):
                at = r * KVH + g
                mixed = factors[0][:, g : g + 1] * keep[j, at].astype(jnp.float32)
                mixed = mixed + factors[1][:, g : g + 1] * got[j, at].astype(jnp.float32)
                out[at] = mixed.astype(jnp.bfloat16)


def fold(rows, keep, got):
    piece = jax.ShapeDtypeStruct(keep.shape[1:], keep.dtype)
    return pl.pallas_call(
        functools.partial(fold_kernel, rows),
        out_shape=(piece,) * keep.shape[0],
        in_specs=[whole(VMEM)] * 2,
        out_specs=(whole(VMEM),) * keep.shape[0],
        compiler_params=pltpu.CompilerParams(vmem_limit_bytes=LIMIT),
        cost_estimate=pl.CostEstimate(
            flops=keep.size * 4, transcendentals=0, bytes_accessed=keep.size * 6
        ),
        name="fold",
    )(keep, got)


def settle_kernel(pieces, source, out, sems):
    step = source.shape[0] // pieces
    spans = [pl.ds(i * step, step) for i in range(pieces)]
    puts = [
        pltpu.make_async_copy(source.at[span], out.at[span], sems.at[i])
        for i, span in enumerate(spans)
    ]
    for put in puts:
        put.start()
    for put in puts:
        put.wait()


def settle(source):
    pieces = 4
    return pl.pallas_call(
        functools.partial(settle_kernel, pieces),
        out_shape=jax.ShapeDtypeStruct(source.shape, source.dtype),
        in_specs=[whole(VMEM)],
        out_specs=whole(pl.ANY),
        scratch_shapes=[pltpu.SemaphoreType.DMA((pieces,))],
        cost_estimate=pl.CostEstimate(
            flops=0, transcendentals=0, bytes_accessed=2 * source.size * 2
        ),
        name="settle",
    )(source)


def merge_kernel(rows_p, rows_d, message, new_k, new_v, *refs):
    parts, (prefill_out, decode_out, lines) = refs[:-3], refs[-3:]
    sources = len(parts)
    rows = rows_p + rows_d
    lane = lax.broadcasted_iota(jnp.int32, (GRP, 128), 1)
    for r in range(rows):
        raw = [part[rows * KVH + r].astype(jnp.float32) for part in parts]
        high = functools.reduce(jnp.maximum, raw)
        fresh = []
        if r >= rows_p:
            request, step = divmod(r - rows_p, STEPS)
            for t in range(step + 1):
                score = jnp.zeros((GRP, 128), jnp.float32)
                for g in range(KVH):
                    query = message[r * KVH + g].astype(jnp.float32)
                    at = request * STEPS + t
                    key = new_k[at : at + 1, g * HD : (g + 1) * HD].astype(jnp.float32)
                    column = jnp.sum(query * key, axis=1, keepdims=True) * (HD ** (-0.5))
                    score = jnp.where(lane == g, column, score)
                fresh.append((request * STEPS + t, score))
                high = jnp.maximum(high, score)
        high = jnp.where(lane < KVH, high, 0.0)
        total = jnp.zeros((GRP, 128), jnp.float32)
        factors = []
        for s in range(sources):
            factor = jnp.exp(jnp.where(lane < KVH, raw[s], 0.0) - high)
            size = pltpu.roll(raw[s], 128 - KVH, 1) + pltpu.roll(raw[s], 128 - 2 * KVH, 1)
            total = total + factor * size
            factors.append(factor)
        fresh = [(at, jnp.exp(score - high)) for at, score in fresh]
        for _, weight in fresh:
            total = total + weight
        total = jnp.where(lane < KVH, total, 1.0)
        factors = [factor / total for factor in factors]
        fresh = [
            (at, (weight / total).astype(jnp.bfloat16).astype(jnp.float32)) for at, weight in fresh
        ]
        for g in range(KVH):
            result = jnp.zeros((GRP, HD), jnp.float32)
            for s in range(sources):
                block = parts[s][r * KVH + g].astype(jnp.float32)
                result = result + factors[s][:, g : g + 1] * block
            for at, weight in fresh:
                value = new_v[at : at + 1, g * HD : (g + 1) * HD].astype(jnp.float32)
                result = result + weight[:, g : g + 1] * value
            for h in range(GRP):
                column = (g * GRP + h) * HD
                lines[r : r + 1, column : column + HD] = result[h : h + 1, :]
    prefill_out[...] = lines[0:rows_p, :].astype(jnp.bfloat16)
    decode_out[...] = lines[rows_p:rows, :].astype(jnp.bfloat16)


def merge(rows_p, rows_d, parts, message, new_k, new_v):
    rows = rows_p + rows_d
    return pl.pallas_call(
        functools.partial(merge_kernel, rows_p, rows_d),
        out_shape=(
            jax.ShapeDtypeStruct((rows_p, HQ * HD), jnp.bfloat16),
            jax.ShapeDtypeStruct((rows_d, HQ * HD), jnp.bfloat16),
        ),
        in_specs=[whole(VMEM)] * (3 + len(parts)),
        out_specs=(whole(VMEM), whole(VMEM)),
        scratch_shapes=[pltpu.VMEM((rows, HQ * HD), jnp.float32)],
        compiler_params=pltpu.CompilerParams(vmem_limit_bytes=LIMIT),
        cost_estimate=pl.CostEstimate(
            flops=len(parts) * parts[0].size * 4,
            transcendentals=0,
            bytes_accessed=len(parts) * parts[0].size * 2,
        ),
        name="merge",
    )(message, new_k.reshape(rows_d, KVD), new_v.reshape(rows_d, KVD), *parts)


def swap(array, distance):
    shards = lax.axis_size("seq")
    return lax.ppermute(array, "seq", [(i, i ^ distance) for i in range(shards)])


def exchange(array):
    return lax.all_to_all(array, "seq", split_axis=0, concat_axis=0, tiled=True)


def per_device(
    prefill_q, cache_k, cache_v, page_counts, page_owner, decode_q, decode_k, decode_v, context_len
):
    shards = lax.axis_size("seq")
    page_slots = cache_k.shape[0] // PAGE
    capacity = max(2, 2 * page_slots // shards)
    rows_p = prefill_q.shape[0]
    rows_d = decode_q.shape[0] * STEPS
    owners = page_owner.reshape(-1)
    pages_k = cache_k.reshape(page_slots, PAGE, KVD)
    pages_v = cache_v.reshape(page_slots, PAGE, KVD)
    rows = rows_p + rows_d
    message = make_message(prefill_q, decode_q, page_owner, context_len)
    far = [message]
    for k in range(4, shards, 4):
        far.append(swap(message, k))
    packed_k = pack(owners, page_counts, pages_k, shards, capacity)
    packed_v = pack(owners, page_counts, pages_v, shards, capacity)
    own = jnp.concatenate(far, axis=0)
    across = swap(own, 2)
    beside = swap(own, 1)
    corner = swap(across, 1)
    store_k = exchange(packed_k)
    keep, give, table = attend(
        rows_p,
        rows_d,
        capacity,
        page_counts,
        (own, beside, across, corner),
        cache_k,
        cache_v,
    )
    got = swap(give, 1)
    folded = fold(rows, keep, got)
    parts = [folded[0]]
    for j in range(1, shards // 2):
        parts.append(swap(folded[j], 2 * j))
    packed_v, store_k = lax.optimization_barrier((packed_v, store_k))
    store_v = exchange(packed_v)
    prefill_out, decode_out = merge(rows_p, rows_d, parts, message, decode_k, decode_v)
    store_k = settle(store_k)
    store_v = settle(store_v)
    store_page = table[:, :capacity].reshape(-1)
    return (
        prefill_out,
        decode_out.reshape(decode_q.shape),
        store_k.reshape(-1, KVD),
        store_v.reshape(-1, KVD),
        store_page,
    )


def solution(mesh):
    in_specs = (
        P(("groups", "seq"), None),
        P(("groups", "seq"), None),
        P(("groups", "seq"), None),
        P("groups"),
        P(("groups", "seq"), None),
        P(("groups", "seq"), None, None),
        P(("groups", "seq"), None, None),
        P(("groups", "seq"), None, None),
        P(("groups", "seq")),
    )
    out_specs = (
        P(("groups", "seq"), None),
        P(("groups", "seq"), None, None),
        P(("groups", "seq"), None),
        P(("groups", "seq"), None),
        P(("groups", "seq")),
    )
    return jax.shard_map(
        per_device, mesh=mesh, in_specs=in_specs, out_specs=out_specs, check_vma=False
    )
```

```python
import functools
import jax
import jax.numpy as jnp
from jax import lax
from jax.experimental import pallas as pl
from jax.experimental.pallas import tpu as pltpu
from jax.sharding import PartitionSpec as P

HQ = 64
KVH = 8
HD = 128
PAGE = 8
STEPS = 2
KVD = 1024
GRP = HQ // KVH
MASKED = -1e30
VMEM = pltpu.MemorySpace.VMEM
SMEM = pltpu.MemorySpace.SMEM
LIMIT = 32 * 1024 * 1024
SMALL = 8 * 1024 * 1024


def whole(space):
    return pl.BlockSpec(memory_space=space)


def message_kernel(rows_p, rows_d, length, prefill_q, decode_q, owners, out, rows):
    for r in range(rows_p + rows_d):
        ref, at = (prefill_q, r) if r < rows_p else (decode_q, r - rows_p)
        line = ref[at : at + 1, :].astype(jnp.float32)
        for h in range(HQ):
            rows[r * HQ + h : r * HQ + h + 1, :] = line[:, h * HD : (h + 1) * HD]
    base = (rows_p + rows_d) * HQ
    slots = owners.shape[1]
    rows[base : base + 8, :] = jnp.zeros((8, 128), jnp.float32)
    rows[base : base + 1, 0:slots] = owners[...].astype(jnp.float32)
    lane = lax.broadcasted_iota(jnp.int32, (1, 128), 1)
    digits = jnp.zeros((1, 128), jnp.int32)
    for q in range(length.shape[0]):
        value = length[q]
        digits = jnp.where(lane == 2 * q, value // 256, digits)
        digits = jnp.where(lane == 2 * q + 1, value % 256, digits)
    rows[base + 1 : base + 2, :] = digits.astype(jnp.float32)
    out[...] = rows[...].reshape(out.shape).astype(jnp.bfloat16)


def make_message(prefill_q, decode_q, page_owner, context_len):
    rows_p = prefill_q.shape[0]
    rows_d = decode_q.shape[0] * STEPS
    blocks = (rows_p + rows_d) * KVH + 1
    return pl.pallas_call(
        functools.partial(message_kernel, rows_p, rows_d),
        out_shape=jax.ShapeDtypeStruct((blocks, 8, 128), jnp.bfloat16),
        in_specs=[whole(SMEM), whole(VMEM), whole(VMEM), whole(VMEM)],
        out_specs=whole(VMEM),
        scratch_shapes=[pltpu.VMEM((blocks * 8, 128), jnp.float32)],
        compiler_params=pltpu.CompilerParams(vmem_limit_bytes=SMALL),
        name="message",
    )(context_len, prefill_q, decode_q.reshape(rows_d, HQ * HD), page_owner.reshape(1, -1))


def pack_kernel(shards, first, depth, owners, counts, pages, out, taken):
    me = lax.axis_index("seq")
    blank = jnp.zeros(pages.shape[1:], pages.dtype)

    def reset(o, carry):
        taken[o] = 0
        return carry

    lax.fori_loop(0, shards, reset, 0)

    def clear(i, carry):
        out[i] = blank
        return carry

    lax.fori_loop(0, shards * depth, clear, 0, unroll=4)

    def place(j, carry):
        o = owners[j]
        k = taken[o] - first
        taken[o] = k + first + 1

        @pl.when((k >= 0) & (k < depth))
        def _():
            out[o * depth + k] = pages[j]

        return carry

    lax.fori_loop(0, counts[me], place, 0)


def pack(owners, counts, pages, shards, first, depth, limit=None):
    slots = pages.shape[0]
    return pl.pallas_call(
        functools.partial(pack_kernel, shards, first, depth),
        out_shape=jax.ShapeDtypeStruct((shards * depth, PAGE, KVD), pages.dtype),
        in_specs=[whole(SMEM), whole(SMEM), whole(VMEM)],
        out_specs=whole(VMEM),
        scratch_shapes=[pltpu.SMEM((shards,), jnp.int32)],
        compiler_params=pltpu.CompilerParams(vmem_limit_bytes=limit),
        cost_estimate=pl.CostEstimate(
            flops=0,
            transcendentals=0,
            bytes_accessed=(slots + shards * depth) * PAGE * KVD * 2,
        ),
        name="pack",
    )(owners, counts, pages)


def attend_kernel(rows_p, rows_d, capacity, counts, *refs):
    messages, refs = refs[:4], refs[4:]
    keys, values, keep, give, table, limits, stats, hits = refs
    me = lax.axis_index("seq")
    rows = rows_p + rows_d
    blocks = rows * KVH + 1
    shards = 4 * messages[0].shape[0] // blocks
    height = shards * rows * GRP
    held = keys.shape[0]

    def block(k, at):
        return messages[k % 4][(k // 4) * blocks + at]

    def count(d, carry):
        before, total = carry
        here = counts[d]
        return (before + jnp.where(d < me, here, 0), total + here)

    before, total = lax.fori_loop(0, shards, count, (jnp.int32(0), jnp.int32(0)))
    start = PAGE * before
    live = PAGE * counts[me]
    first = PAGE * total - shards * rows_p + 1
    lane = lax.broadcasted_iota(jnp.int32, (1, 128), 1)
    for k in range(shards):
        d = me ^ k
        tail = block(k, rows * KVH).astype(jnp.float32)
        for r in range(rows):
            at = (k * rows + r) * GRP
            if r < rows_p:
                bound = jnp.minimum(first + d * rows_p + r - start, live)
                limits[at : at + GRP, :] = jnp.full((GRP, 128), bound, jnp.int32)
            else:
                q = (r - rows_p) // STEPS
                length = tail[1:2, 2 * q : 2 * q + 1] * 256.0 + tail[1:2, 2 * q + 1 : 2 * q + 2]
                bound = jnp.minimum(length.astype(jnp.int32) - start, live)
                limits[at : at + GRP, :] = jnp.broadcast_to(bound, (GRP, 128))
        hit = (tail[0:1, :].astype(jnp.int32) == me) & (lane < counts[d])
        hits[pl.ds(d, 1), :] = hit.astype(jnp.float32)

    hit = hits[...]
    earlier = (
        lax.broadcasted_iota(jnp.int32, (128, 128), 0)
        < lax.broadcasted_iota(jnp.int32, (128, 128), 1)
    ).astype(jnp.bfloat16)
    rank = jnp.dot(hit.astype(jnp.bfloat16), earlier, preferred_element_type=jnp.float32)
    wide = lax.broadcasted_iota(jnp.int32, hit.shape, 1)
    depth = lax.broadcasted_iota(jnp.int32, hit.shape, 0)
    numbered = jnp.zeros(hit.shape, jnp.float32)
    for k in range(capacity):
        match = jnp.where((hit > 0.5) & (rank == float(k)), (wide + 1).astype(jnp.float32), 0.0)
        found = jnp.sum(match, axis=1, keepdims=True)
        numbered = jnp.where(wide == k, found, numbered)
    within = numbered.astype(jnp.int32)
    slots = held // PAGE
    table[...] = jnp.where(within > 0, depth * slots + within - 1, -1)

    stats[...] = jnp.zeros_like(stats)
    spot = lax.broadcasted_iota(jnp.int32, (height, 128), 1)
    column = lax.broadcasted_iota(jnp.int32, (height, held), 1)
    pieces = [(k, r, (k * rows + r) * GRP) for k in range(shards) for r in range(rows)]

    def target(k):
        return give if k % 2 else keep

    def one_group(g, carry):
        query = jnp.concatenate(
            [block(k, r * KVH + g).astype(jnp.float32) for k, r, _ in pieces], axis=0
        ).astype(jnp.bfloat16)
        across = pl.ds(pl.multiple_of(g * HD, HD), HD)
        scores = lax.dot_general(
            query, keys[:, across], (((1,), (1,)), ((), ())), preferred_element_type=jnp.float32
        ) * (HD ** (-0.5))
        allowed = column < jnp.concatenate([limits[...]] * (held // 128), axis=1)
        scores = jnp.where(allowed, scores, MASKED)
        high = jnp.max(scores, axis=1, keepdims=True).astype(jnp.bfloat16).astype(jnp.float32)
        weights = jnp.where(allowed, jnp.exp(scores - high), 0.0)
        total = jnp.sum(weights, axis=1, keepdims=True)
        product = jnp.dot(
            weights.astype(jnp.bfloat16), values[:, across], preferred_element_type=jnp.float32
        )
        coarse = total.astype(jnp.bfloat16).astype(jnp.float32)
        kept = jnp.where(spot == g, high, stats[...])
        kept = jnp.where(spot == KVH + g, coarse, kept)
        stats[...] = jnp.where(spot == 2 * KVH + g, total - coarse, kept)
        for k, r, at in pieces:
            target(k)[k // 2, r * KVH + g] = product[at : at + GRP, :].astype(jnp.bfloat16)
        return carry

    lax.fori_loop(0, KVH, one_group, 0)
    for k, r, at in pieces:
        target(k)[k // 2, rows * KVH + r] = stats[at : at + GRP, :].astype(jnp.bfloat16)


def attend(rows_p, rows_d, capacity, counts, messages, keys, values):
    rows = rows_p + rows_d
    shards = 4 * messages[0].shape[0] // (rows * KVH + 1)
    height = shards * rows * GRP
    held = keys.shape[0]
    half = jax.ShapeDtypeStruct((shards // 2, rows * (KVH + 1), GRP, 128), jnp.bfloat16)
    return pl.pallas_call(
        functools.partial(attend_kernel, rows_p, rows_d, capacity),
        out_shape=(half, half, jax.ShapeDtypeStruct((shards, 128), jnp.int32)),
        in_specs=[whole(SMEM)] + [whole(VMEM)] * 6,
        out_specs=(whole(VMEM),) * 3,
        scratch_shapes=[
            pltpu.VMEM((height, 128), jnp.int32),
            pltpu.VMEM((height, 128), jnp.float32),
            pltpu.VMEM((shards, 128), jnp.float32),
        ],
        compiler_params=pltpu.CompilerParams(vmem_limit_bytes=LIMIT),
        cost_estimate=pl.CostEstimate(
            flops=4 * height * KVH * held * HD,
            transcendentals=height * KVH * held,
            bytes_accessed=2 * held * KVD * 2 + 4 * height * KVH * HD,
        ),
        name="attend",
    )(counts, *messages, keys, values)


def fold_kernel(rows, keep, got, *outs):
    lane = lax.broadcasted_iota(jnp.int32, (GRP, 128), 1)
    inside = lane < KVH
    for j, out in enumerate(outs):
        for r in range(rows):
            raw = [ref[j, rows * KVH + r].astype(jnp.float32) for ref in (keep, got)]
            high = jnp.maximum(jnp.where(inside, raw[0], 0.0), jnp.where(inside, raw[1], 0.0))
            factors = [jnp.exp(jnp.where(inside, part, 0.0) - high) for part in raw]
            sizes = [
                pltpu.roll(part, 128 - KVH, 1) + pltpu.roll(part, 128 - 2 * KVH, 1) for part in raw
            ]
            total = jnp.where(inside, factors[0] * sizes[0] + factors[1] * sizes[1], 0.0)
            coarse = total.astype(jnp.bfloat16).astype(jnp.float32)
            line = high + pltpu.roll(coarse, KVH, 1) + pltpu.roll(total - coarse, 2 * KVH, 1)
            out[rows * KVH + r] = line.astype(jnp.bfloat16)
            for g in range(KVH):
                at = r * KVH + g
                mixed = factors[0][:, g : g + 1] * keep[j, at].astype(jnp.float32)
                mixed = mixed + factors[1][:, g : g + 1] * got[j, at].astype(jnp.float32)
                out[at] = mixed.astype(jnp.bfloat16)


def fold(rows, keep, got):
    piece = jax.ShapeDtypeStruct(keep.shape[1:], keep.dtype)
    return pl.pallas_call(
        functools.partial(fold_kernel, rows),
        out_shape=(piece,) * keep.shape[0],
        in_specs=[whole(VMEM)] * 2,
        out_specs=(whole(VMEM),) * keep.shape[0],
        compiler_params=pltpu.CompilerParams(vmem_limit_bytes=LIMIT),
        cost_estimate=pl.CostEstimate(
            flops=keep.size * 4, transcendentals=0, bytes_accessed=keep.size * 6
        ),
        name="fold",
    )(keep, got)


def settle_kernel(pieces, source, out, sems):
    step = source.shape[0] // pieces
    spans = [pl.ds(i * step, step) for i in range(pieces)]
    puts = [
        pltpu.make_async_copy(source.at[span], out.at[span], sems.at[i])
        for i, span in enumerate(spans)
    ]
    for put in puts:
        put.start()
    for put in puts:
        put.wait()


def settle(source):
    pieces = 4
    return pl.pallas_call(
        functools.partial(settle_kernel, pieces),
        out_shape=jax.ShapeDtypeStruct(source.shape, source.dtype),
        in_specs=[whole(VMEM)],
        out_specs=whole(pl.ANY),
        scratch_shapes=[pltpu.SemaphoreType.DMA((pieces,))],
        compiler_params=pltpu.CompilerParams(vmem_limit_bytes=SMALL),
        cost_estimate=pl.CostEstimate(flops=0, transcendentals=0, bytes_accessed=4 * source.size),
        name="settle",
    )(source)


def join_kernel(*refs):
    sources, (out, held, sems_in, sems_out) = refs[:-4], refs[-4:]
    base = 0
    fetches, puts = [], []
    for i, source in enumerate(sources):
        span = pl.ds(base, source.shape[1])
        fetches.append(pltpu.make_async_copy(source, held.at[:, span], sems_in.at[i]))
        puts.append(pltpu.make_async_copy(held.at[:, span], out.at[:, span], sems_out.at[i]))
        base += source.shape[1]
    for fetch in fetches:
        fetch.start()
    for fetch, put in zip(fetches, puts):
        fetch.wait()
        put.start()
    for put in puts:
        put.wait()


def join(shards, *sources):
    sources = [source.reshape(shards, -1, PAGE, KVD) for source in sources]
    depth = sum(source.shape[1] for source in sources)
    shape = (shards, depth, PAGE, KVD)
    return pl.pallas_call(
        join_kernel,
        out_shape=jax.ShapeDtypeStruct(shape, sources[0].dtype),
        in_specs=[whole(pl.ANY)] * len(sources),
        out_specs=whole(pl.ANY),
        scratch_shapes=[
            pltpu.VMEM(shape, sources[0].dtype),
            pltpu.SemaphoreType.DMA((len(sources),)),
            pltpu.SemaphoreType.DMA((len(sources),)),
        ],
        cost_estimate=pl.CostEstimate(
            flops=0, transcendentals=0, bytes_accessed=4 * shards * depth * PAGE * KVD
        ),
        name="join",
    )(*sources)


def merge_kernel(rows_p, rows_d, message, new_k, new_v, *refs):
    parts, (prefill_out, decode_out, lines) = refs[:-3], refs[-3:]
    sources = len(parts)
    rows = rows_p + rows_d
    lane = lax.broadcasted_iota(jnp.int32, (GRP, 128), 1)
    for r in range(rows):
        raw = [part[rows * KVH + r].astype(jnp.float32) for part in parts]
        high = functools.reduce(jnp.maximum, raw)
        fresh = []
        if r >= rows_p:
            request, step = divmod(r - rows_p, STEPS)
            for t in range(step + 1):
                score = jnp.zeros((GRP, 128), jnp.float32)
                for g in range(KVH):
                    query = message[r * KVH + g].astype(jnp.float32)
                    at = request * STEPS + t
                    key = new_k[at : at + 1, g * HD : (g + 1) * HD].astype(jnp.float32)
                    column = jnp.sum(query * key, axis=1, keepdims=True) * (HD ** (-0.5))
                    score = jnp.where(lane == g, column, score)
                fresh.append((request * STEPS + t, score))
                high = jnp.maximum(high, score)
        high = jnp.where(lane < KVH, high, 0.0)
        total = jnp.zeros((GRP, 128), jnp.float32)
        factors = []
        for s in range(sources):
            factor = jnp.exp(jnp.where(lane < KVH, raw[s], 0.0) - high)
            size = pltpu.roll(raw[s], 128 - KVH, 1) + pltpu.roll(raw[s], 128 - 2 * KVH, 1)
            total = total + factor * size
            factors.append(factor)
        fresh = [(at, jnp.exp(score - high)) for at, score in fresh]
        for _, weight in fresh:
            total = total + weight
        total = jnp.where(lane < KVH, total, 1.0)
        factors = [factor / total for factor in factors]
        fresh = [
            (at, (weight / total).astype(jnp.bfloat16).astype(jnp.float32)) for at, weight in fresh
        ]
        for g in range(KVH):
            result = jnp.zeros((GRP, HD), jnp.float32)
            for s in range(sources):
                block = parts[s][r * KVH + g].astype(jnp.float32)
                result = result + factors[s][:, g : g + 1] * block
            for at, weight in fresh:
                value = new_v[at : at + 1, g * HD : (g + 1) * HD].astype(jnp.float32)
                result = result + weight[:, g : g + 1] * value
            for h in range(GRP):
                column = (g * GRP + h) * HD
                lines[r : r + 1, column : column + HD] = result[h : h + 1, :]
    prefill_out[...] = lines[0:rows_p, :].astype(jnp.bfloat16)
    decode_out[...] = lines[rows_p:rows, :].astype(jnp.bfloat16)


def merge(rows_p, rows_d, parts, message, new_k, new_v):
    rows = rows_p + rows_d
    return pl.pallas_call(
        functools.partial(merge_kernel, rows_p, rows_d),
        out_shape=(
            jax.ShapeDtypeStruct((rows_p, HQ * HD), jnp.bfloat16),
            jax.ShapeDtypeStruct((rows_d, HQ * HD), jnp.bfloat16),
        ),
        in_specs=[whole(VMEM)] * (3 + len(parts)),
        out_specs=(whole(VMEM), whole(VMEM)),
        scratch_shapes=[pltpu.VMEM((rows, HQ * HD), jnp.float32)],
        compiler_params=pltpu.CompilerParams(vmem_limit_bytes=LIMIT),
        cost_estimate=pl.CostEstimate(
            flops=len(parts) * parts[0].size * 4,
            transcendentals=0,
            bytes_accessed=len(parts) * parts[0].size * 2,
        ),
        name="merge",
    )(message, new_k.reshape(rows_d, KVD), new_v.reshape(rows_d, KVD), *parts)


def swap(array, distance):
    shards = lax.axis_size("seq")
    return lax.ppermute(array, "seq", [(i, i ^ distance) for i in range(shards)])


def exchange(array):
    return lax.all_to_all(array, "seq", split_axis=0, concat_axis=0, tiled=True)


def per_device(
    prefill_q, cache_k, cache_v, page_counts, page_owner, decode_q, decode_k, decode_v, context_len
):
    shards = lax.axis_size("seq")
    page_slots = cache_k.shape[0] // PAGE
    capacity = max(2, 2 * page_slots // shards)
    rows_p = prefill_q.shape[0]
    rows_d = decode_q.shape[0] * STEPS
    owners = page_owner.reshape(-1)
    pages_k = cache_k.reshape(page_slots, PAGE, KVD)
    pages_v = cache_v.reshape(page_slots, PAGE, KVD)
    rows = rows_p + rows_d
    lead = max(1, capacity // 4)
    early_k = pack(owners, page_counts, pages_k, shards, 0, lead, SMALL)
    store_k1 = exchange(early_k)
    message = make_message(prefill_q, decode_q, page_owner, context_len)
    far = [message]
    for k in range(4, shards, 4):
        far.append(swap(message, k))
    late_k = pack(owners, page_counts, pages_k, shards, lead, capacity - lead)
    packed_v = pack(owners, page_counts, pages_v, shards, 0, capacity)
    store_k2 = exchange(late_k)
    own = jnp.concatenate(far, axis=0)
    across = swap(own, 2)
    beside = swap(own, 1)
    corner = swap(across, 1)
    keep, give, table = attend(
        rows_p,
        rows_d,
        capacity,
        page_counts,
        (own, beside, across, corner),
        cache_k,
        cache_v,
    )
    got = swap(give, 1)
    folded = fold(rows, keep, got)
    parts = [folded[0]]
    for j in range(1, shards // 2):
        parts.append(swap(folded[j], 2 * j))
    store_v = exchange(packed_v)
    prefill_out, decode_out = merge(rows_p, rows_d, parts, message, decode_k, decode_v)
    store_k = join(shards, store_k1, store_k2)
    store_v = settle(store_v)
    store_page = table[:, :capacity].reshape(-1)
    return (
        prefill_out,
        decode_out.reshape(decode_q.shape),
        store_k.reshape(-1, KVD),
        store_v.reshape(-1, KVD),
        store_page,
    )


def solution(mesh):
    in_specs = (
        P(("groups", "seq"), None),
        P(("groups", "seq"), None),
        P(("groups", "seq"), None),
        P("groups"),
        P(("groups", "seq"), None),
        P(("groups", "seq"), None, None),
        P(("groups", "seq"), None, None),
        P(("groups", "seq"), None, None),
        P(("groups", "seq")),
    )
    out_specs = (
        P(("groups", "seq"), None),
        P(("groups", "seq"), None, None),
        P(("groups", "seq"), None),
        P(("groups", "seq"), None),
        P(("groups", "seq")),
    )
    return jax.shard_map(
        per_device, mesh=mesh, in_specs=in_specs, out_specs=out_specs, check_vma=False
    )
```

```python
import functools
import jax
import jax.numpy as jnp
from jax import lax
from jax.experimental import pallas as pl
from jax.experimental.pallas import tpu as pltpu
from jax.sharding import PartitionSpec as P

HQ = 64
KVH = 8
HD = 128
PAGE = 8
STEPS = 2
KVD = 1024
GRP = HQ // KVH
MASKED = -1e30
VMEM = pltpu.MemorySpace.VMEM
SMEM = pltpu.MemorySpace.SMEM
LIMIT = 32 * 1024 * 1024
SMALL = 8 * 1024 * 1024


def whole(space):
    return pl.BlockSpec(memory_space=space)


def message_kernel(rows_p, rows_d, length, prefill_q, decode_q, owners, out, rows):
    for r in range(rows_p + rows_d):
        ref, at = (prefill_q, r) if r < rows_p else (decode_q, r - rows_p)
        line = ref[at : at + 1, :].astype(jnp.float32)
        for h in range(HQ):
            rows[r * HQ + h : r * HQ + h + 1, :] = line[:, h * HD : (h + 1) * HD]
    base = (rows_p + rows_d) * HQ
    slots = owners.shape[1]
    rows[base : base + 8, :] = jnp.zeros((8, 128), jnp.float32)
    rows[base : base + 1, 0:slots] = owners[...].astype(jnp.float32)
    lane = lax.broadcasted_iota(jnp.int32, (1, 128), 1)
    digits = jnp.zeros((1, 128), jnp.int32)
    for q in range(length.shape[0]):
        value = length[q]
        digits = jnp.where(lane == 2 * q, value // 256, digits)
        digits = jnp.where(lane == 2 * q + 1, value % 256, digits)
    rows[base + 1 : base + 2, :] = digits.astype(jnp.float32)
    out[...] = rows[...].reshape(out.shape).astype(jnp.bfloat16)


def make_message(prefill_q, decode_q, page_owner, context_len):
    rows_p = prefill_q.shape[0]
    rows_d = decode_q.shape[0] * STEPS
    blocks = (rows_p + rows_d) * KVH + 1
    return pl.pallas_call(
        functools.partial(message_kernel, rows_p, rows_d),
        out_shape=jax.ShapeDtypeStruct((blocks, 8, 128), jnp.bfloat16),
        in_specs=[whole(SMEM), whole(VMEM), whole(VMEM), whole(VMEM)],
        out_specs=whole(VMEM),
        scratch_shapes=[pltpu.VMEM((blocks * 8, 128), jnp.float32)],
        compiler_params=pltpu.CompilerParams(vmem_limit_bytes=SMALL),
        name="message",
    )(context_len, prefill_q, decode_q.reshape(rows_d, HQ * HD), page_owner.reshape(1, -1))


def pack_kernel(shards, first, depth, owners, counts, pages, out, taken):
    me = lax.axis_index("seq")
    blank = jnp.zeros(pages.shape[1:], pages.dtype)

    def reset(o, carry):
        taken[o] = 0
        return carry

    lax.fori_loop(0, shards, reset, 0)

    def clear(i, carry):
        out[i] = blank
        return carry

    lax.fori_loop(0, shards * depth, clear, 0, unroll=4)

    def place(j, carry):
        o = owners[j]
        k = taken[o] - first
        taken[o] = k + first + 1

        @pl.when((k >= 0) & (k < depth))
        def _():
            out[o * depth + k] = pages[j]

        return carry

    lax.fori_loop(0, counts[me], place, 0)


def pack(owners, counts, pages, shards, first, depth, limit=None):
    slots = pages.shape[0]
    return pl.pallas_call(
        functools.partial(pack_kernel, shards, first, depth),
        out_shape=jax.ShapeDtypeStruct((shards * depth, PAGE, KVD), pages.dtype),
        in_specs=[whole(SMEM), whole(SMEM), whole(VMEM)],
        out_specs=whole(VMEM),
        scratch_shapes=[pltpu.SMEM((shards,), jnp.int32)],
        compiler_params=pltpu.CompilerParams(vmem_limit_bytes=limit),
        cost_estimate=pl.CostEstimate(
            flops=0,
            transcendentals=0,
            bytes_accessed=(slots + shards * depth) * PAGE * KVD * 2,
        ),
        name="pack",
    )(owners, counts, pages)


def attend_kernel(rows_p, rows_d, capacity, counts, *refs):
    messages, refs = refs[:4], refs[4:]
    keys, values, keep, give, table, limits, stats, hits = refs
    me = lax.axis_index("seq")
    rows = rows_p + rows_d
    blocks = rows * KVH + 1
    shards = 4 * messages[0].shape[0] // blocks
    height = shards * rows * GRP
    held = keys.shape[0]

    def block(k, at):
        return messages[k % 4][(k // 4) * blocks + at]

    def count(d, carry):
        before, total = carry
        here = counts[d]
        return (before + jnp.where(d < me, here, 0), total + here)

    before, total = lax.fori_loop(0, shards, count, (jnp.int32(0), jnp.int32(0)))
    start = PAGE * before
    live = PAGE * counts[me]
    first = PAGE * total - shards * rows_p + 1
    lane = lax.broadcasted_iota(jnp.int32, (1, 128), 1)
    for k in range(shards):
        d = me ^ k
        tail = block(k, rows * KVH).astype(jnp.float32)
        for r in range(rows):
            at = (k * rows + r) * GRP
            if r < rows_p:
                bound = jnp.minimum(first + d * rows_p + r - start, live)
                limits[at : at + GRP, :] = jnp.full((GRP, 128), bound, jnp.int32)
            else:
                q = (r - rows_p) // STEPS
                length = tail[1:2, 2 * q : 2 * q + 1] * 256.0 + tail[1:2, 2 * q + 1 : 2 * q + 2]
                bound = jnp.minimum(length.astype(jnp.int32) - start, live)
                limits[at : at + GRP, :] = jnp.broadcast_to(bound, (GRP, 128))
        hit = (tail[0:1, :].astype(jnp.int32) == me) & (lane < counts[d])
        hits[pl.ds(d, 1), :] = hit.astype(jnp.float32)

    hit = hits[...]
    earlier = (
        lax.broadcasted_iota(jnp.int32, (128, 128), 0)
        < lax.broadcasted_iota(jnp.int32, (128, 128), 1)
    ).astype(jnp.bfloat16)
    rank = jnp.dot(hit.astype(jnp.bfloat16), earlier, preferred_element_type=jnp.float32)
    wide = lax.broadcasted_iota(jnp.int32, hit.shape, 1)
    depth = lax.broadcasted_iota(jnp.int32, hit.shape, 0)
    numbered = jnp.zeros(hit.shape, jnp.float32)
    for k in range(capacity):
        match = jnp.where((hit > 0.5) & (rank == float(k)), (wide + 1).astype(jnp.float32), 0.0)
        found = jnp.sum(match, axis=1, keepdims=True)
        numbered = jnp.where(wide == k, found, numbered)
    within = numbered.astype(jnp.int32)
    slots = held // PAGE
    table[...] = jnp.where(within > 0, depth * slots + within - 1, -1)

    stats[...] = jnp.zeros_like(stats)
    spot = lax.broadcasted_iota(jnp.int32, (height, 128), 1)
    column = lax.broadcasted_iota(jnp.int32, (height, held), 1)
    pieces = [(k, r, (k * rows + r) * GRP) for k in range(shards) for r in range(rows)]

    def target(k):
        return give if k % 2 else keep

    def one_group(g, carry):
        query = jnp.concatenate(
            [block(k, r * KVH + g).astype(jnp.float32) for k, r, _ in pieces], axis=0
        ).astype(jnp.bfloat16)
        across = pl.ds(pl.multiple_of(g * HD, HD), HD)
        scores = lax.dot_general(
            query, keys[:, across], (((1,), (1,)), ((), ())), preferred_element_type=jnp.float32
        ) * (HD ** (-0.5))
        allowed = column < jnp.concatenate([limits[...]] * (held // 128), axis=1)
        scores = jnp.where(allowed, scores, MASKED)
        high = jnp.max(scores, axis=1, keepdims=True).astype(jnp.bfloat16).astype(jnp.float32)
        weights = jnp.where(allowed, jnp.exp(scores - high), 0.0)
        total = jnp.sum(weights, axis=1, keepdims=True)
        product = jnp.dot(
            weights.astype(jnp.bfloat16), values[:, across], preferred_element_type=jnp.float32
        )
        coarse = total.astype(jnp.bfloat16).astype(jnp.float32)
        kept = jnp.where(spot == g, high, stats[...])
        kept = jnp.where(spot == KVH + g, coarse, kept)
        stats[...] = jnp.where(spot == 2 * KVH + g, total - coarse, kept)
        for k, r, at in pieces:
            target(k)[k // 2, r * KVH + g] = product[at : at + GRP, :].astype(jnp.bfloat16)
        return carry

    lax.fori_loop(0, KVH, one_group, 0)
    for k, r, at in pieces:
        target(k)[k // 2, rows * KVH + r] = stats[at : at + GRP, :].astype(jnp.bfloat16)


def attend(rows_p, rows_d, capacity, counts, messages, keys, values):
    rows = rows_p + rows_d
    shards = 4 * messages[0].shape[0] // (rows * KVH + 1)
    height = shards * rows * GRP
    held = keys.shape[0]
    half = jax.ShapeDtypeStruct((shards // 2, rows * (KVH + 1), GRP, 128), jnp.bfloat16)
    return pl.pallas_call(
        functools.partial(attend_kernel, rows_p, rows_d, capacity),
        out_shape=(half, half, jax.ShapeDtypeStruct((shards, 128), jnp.int32)),
        in_specs=[whole(SMEM)] + [whole(VMEM)] * 6,
        out_specs=(whole(VMEM),) * 3,
        scratch_shapes=[
            pltpu.VMEM((height, 128), jnp.int32),
            pltpu.VMEM((height, 128), jnp.float32),
            pltpu.VMEM((shards, 128), jnp.float32),
        ],
        compiler_params=pltpu.CompilerParams(vmem_limit_bytes=LIMIT),
        cost_estimate=pl.CostEstimate(
            flops=4 * height * KVH * held * HD,
            transcendentals=height * KVH * held,
            bytes_accessed=2 * held * KVD * 2 + 4 * height * KVH * HD,
        ),
        name="attend",
    )(counts, *messages, keys, values)


def fold_kernel(rows, keep, got, *outs):
    lane = lax.broadcasted_iota(jnp.int32, (GRP, 128), 1)
    inside = lane < KVH
    for j, out in enumerate(outs):
        for r in range(rows):
            raw = [ref[j, rows * KVH + r].astype(jnp.float32) for ref in (keep, got)]
            high = jnp.maximum(jnp.where(inside, raw[0], 0.0), jnp.where(inside, raw[1], 0.0))
            factors = [jnp.exp(jnp.where(inside, part, 0.0) - high) for part in raw]
            sizes = [
                pltpu.roll(part, 128 - KVH, 1) + pltpu.roll(part, 128 - 2 * KVH, 1) for part in raw
            ]
            total = jnp.where(inside, factors[0] * sizes[0] + factors[1] * sizes[1], 0.0)
            coarse = total.astype(jnp.bfloat16).astype(jnp.float32)
            line = high + pltpu.roll(coarse, KVH, 1) + pltpu.roll(total - coarse, 2 * KVH, 1)
            out[rows * KVH + r] = line.astype(jnp.bfloat16)
            for g in range(KVH):
                at = r * KVH + g
                mixed = factors[0][:, g : g + 1] * keep[j, at].astype(jnp.float32)
                mixed = mixed + factors[1][:, g : g + 1] * got[j, at].astype(jnp.float32)
                out[at] = mixed.astype(jnp.bfloat16)


def fold(rows, keep, got):
    piece = jax.ShapeDtypeStruct(keep.shape[1:], keep.dtype)
    return pl.pallas_call(
        functools.partial(fold_kernel, rows),
        out_shape=(piece,) * keep.shape[0],
        in_specs=[whole(VMEM)] * 2,
        out_specs=(whole(VMEM),) * keep.shape[0],
        compiler_params=pltpu.CompilerParams(vmem_limit_bytes=LIMIT),
        cost_estimate=pl.CostEstimate(
            flops=keep.size * 4, transcendentals=0, bytes_accessed=keep.size * 6
        ),
        name="fold",
    )(keep, got)


def settle_kernel(pieces, source, out, sems):
    step = source.shape[0] // pieces
    spans = [pl.ds(i * step, step) for i in range(pieces)]
    puts = [
        pltpu.make_async_copy(source.at[span], out.at[span], sems.at[i])
        for i, span in enumerate(spans)
    ]
    for put in puts:
        put.start()
    for put in puts:
        put.wait()


def settle(source):
    pieces = 4
    return pl.pallas_call(
        functools.partial(settle_kernel, pieces),
        out_shape=jax.ShapeDtypeStruct(source.shape, source.dtype),
        in_specs=[whole(VMEM)],
        out_specs=whole(pl.ANY),
        scratch_shapes=[pltpu.SemaphoreType.DMA((pieces,))],
        compiler_params=pltpu.CompilerParams(vmem_limit_bytes=SMALL),
        cost_estimate=pl.CostEstimate(flops=0, transcendentals=0, bytes_accessed=4 * source.size),
        name="settle",
    )(source)


def join_kernel(*refs):
    sources, (out, held, sems_in, sems_out) = refs[:-4], refs[-4:]
    base = 0
    fetches, puts = [], []
    for i, source in enumerate(sources):
        span = pl.ds(base, source.shape[1])
        fetches.append(pltpu.make_async_copy(source, held.at[:, span], sems_in.at[i]))
        puts.append(pltpu.make_async_copy(held.at[:, span], out.at[:, span], sems_out.at[i]))
        base += source.shape[1]
    for fetch in fetches:
        fetch.start()
    for fetch, put in zip(fetches, puts):
        fetch.wait()
        put.start()
    for put in puts:
        put.wait()


def join(shards, *sources):
    sources = [source.reshape(shards, -1, PAGE, KVD) for source in sources]
    depth = sum(source.shape[1] for source in sources)
    shape = (shards, depth, PAGE, KVD)
    return pl.pallas_call(
        join_kernel,
        out_shape=jax.ShapeDtypeStruct(shape, sources[0].dtype),
        in_specs=[whole(pl.ANY)] * len(sources),
        out_specs=whole(pl.ANY),
        scratch_shapes=[
            pltpu.VMEM(shape, sources[0].dtype),
            pltpu.SemaphoreType.DMA((len(sources),)),
            pltpu.SemaphoreType.DMA((len(sources),)),
        ],
        cost_estimate=pl.CostEstimate(
            flops=0, transcendentals=0, bytes_accessed=4 * shards * depth * PAGE * KVD
        ),
        name="join",
    )(*sources)


def merge_kernel(rows_p, rows_d, message, new_k, new_v, *refs):
    parts, (prefill_out, decode_out, lines) = refs[:-3], refs[-3:]
    sources = len(parts)
    rows = rows_p + rows_d
    lane = lax.broadcasted_iota(jnp.int32, (GRP, 128), 1)
    for r in range(rows):
        raw = [part[rows * KVH + r].astype(jnp.float32) for part in parts]
        high = functools.reduce(jnp.maximum, raw)
        fresh = []
        if r >= rows_p:
            request, step = divmod(r - rows_p, STEPS)
            for t in range(step + 1):
                score = jnp.zeros((GRP, 128), jnp.float32)
                for g in range(KVH):
                    query = message[r * KVH + g].astype(jnp.float32)
                    at = request * STEPS + t
                    key = new_k[at : at + 1, g * HD : (g + 1) * HD].astype(jnp.float32)
                    column = jnp.sum(query * key, axis=1, keepdims=True) * (HD ** (-0.5))
                    score = jnp.where(lane == g, column, score)
                fresh.append((request * STEPS + t, score))
                high = jnp.maximum(high, score)
        high = jnp.where(lane < KVH, high, 0.0)
        total = jnp.zeros((GRP, 128), jnp.float32)
        factors = []
        for s in range(sources):
            factor = jnp.exp(jnp.where(lane < KVH, raw[s], 0.0) - high)
            size = pltpu.roll(raw[s], 128 - KVH, 1) + pltpu.roll(raw[s], 128 - 2 * KVH, 1)
            total = total + factor * size
            factors.append(factor)
        fresh = [(at, jnp.exp(score - high)) for at, score in fresh]
        for _, weight in fresh:
            total = total + weight
        total = jnp.where(lane < KVH, total, 1.0)
        factors = [factor / total for factor in factors]
        fresh = [
            (at, (weight / total).astype(jnp.bfloat16).astype(jnp.float32)) for at, weight in fresh
        ]
        for g in range(KVH):
            result = jnp.zeros((GRP, HD), jnp.float32)
            for s in range(sources):
                block = parts[s][r * KVH + g].astype(jnp.float32)
                result = result + factors[s][:, g : g + 1] * block
            for at, weight in fresh:
                value = new_v[at : at + 1, g * HD : (g + 1) * HD].astype(jnp.float32)
                result = result + weight[:, g : g + 1] * value
            for h in range(GRP):
                column = (g * GRP + h) * HD
                lines[r : r + 1, column : column + HD] = result[h : h + 1, :]
    prefill_out[...] = lines[0:rows_p, :].astype(jnp.bfloat16)
    decode_out[...] = lines[rows_p:rows, :].astype(jnp.bfloat16)


def merge(rows_p, rows_d, parts, message, new_k, new_v):
    rows = rows_p + rows_d
    return pl.pallas_call(
        functools.partial(merge_kernel, rows_p, rows_d),
        out_shape=(
            jax.ShapeDtypeStruct((rows_p, HQ * HD), jnp.bfloat16),
            jax.ShapeDtypeStruct((rows_d, HQ * HD), jnp.bfloat16),
        ),
        in_specs=[whole(VMEM)] * (3 + len(parts)),
        out_specs=(whole(VMEM), whole(VMEM)),
        scratch_shapes=[pltpu.VMEM((rows, HQ * HD), jnp.float32)],
        compiler_params=pltpu.CompilerParams(vmem_limit_bytes=LIMIT),
        cost_estimate=pl.CostEstimate(
            flops=len(parts) * parts[0].size * 4,
            transcendentals=0,
            bytes_accessed=len(parts) * parts[0].size * 2,
        ),
        name="merge",
    )(message, new_k.reshape(rows_d, KVD), new_v.reshape(rows_d, KVD), *parts)


def swap(array, distance):
    shards = lax.axis_size("seq")
    return lax.ppermute(array, "seq", [(i, i ^ distance) for i in range(shards)])


def exchange(array):
    return lax.all_to_all(array, "seq", split_axis=0, concat_axis=0, tiled=True)


def per_device(
    prefill_q, cache_k, cache_v, page_counts, page_owner, decode_q, decode_k, decode_v, context_len
):
    shards = lax.axis_size("seq")
    page_slots = cache_k.shape[0] // PAGE
    capacity = max(2, 2 * page_slots // shards)
    rows_p = prefill_q.shape[0]
    rows_d = decode_q.shape[0] * STEPS
    owners = page_owner.reshape(-1)
    pages_k = cache_k.reshape(page_slots, PAGE, KVD)
    pages_v = cache_v.reshape(page_slots, PAGE, KVD)
    rows = rows_p + rows_d
    message = make_message(prefill_q, decode_q, page_owner, context_len)
    far = [message]
    for k in range(4, shards, 4):
        far.append(swap(message, k))
    packed_k = pack(owners, page_counts, pages_k, shards, 0, capacity)
    store_k = exchange(packed_k)
    packed_v = pack(owners, page_counts, pages_v, shards, 0, capacity)
    own = jnp.concatenate(far, axis=0)
    across = swap(own, 2)
    beside = swap(own, 1)
    corner = swap(across, 1)
    keep, give, table = attend(
        rows_p,
        rows_d,
        capacity,
        page_counts,
        (own, beside, across, corner),
        cache_k,
        cache_v,
    )
    got = swap(give, 1)
    folded = fold(rows, keep, got)
    parts = [folded[0]]
    for j in range(1, shards // 2):
        parts.append(swap(folded[j], 2 * j))
    store_v = exchange(packed_v)
    prefill_out, decode_out = merge(rows_p, rows_d, parts, message, decode_k, decode_v)
    store_k = join(shards, store_k)
    store_v = settle(store_v)
    store_page = table[:, :capacity].reshape(-1)
    return (
        prefill_out,
        decode_out.reshape(decode_q.shape),
        store_k.reshape(-1, KVD),
        store_v.reshape(-1, KVD),
        store_page,
    )


def solution(mesh):
    in_specs = (
        P(("groups", "seq"), None),
        P(("groups", "seq"), None),
        P(("groups", "seq"), None),
        P("groups"),
        P(("groups", "seq"), None),
        P(("groups", "seq"), None, None),
        P(("groups", "seq"), None, None),
        P(("groups", "seq"), None, None),
        P(("groups", "seq")),
    )
    out_specs = (
        P(("groups", "seq"), None),
        P(("groups", "seq"), None, None),
        P(("groups", "seq"), None),
        P(("groups", "seq"), None),
        P(("groups", "seq")),
    )
    return jax.shard_map(
        per_device, mesh=mesh, in_specs=in_specs, out_specs=out_specs, check_vma=False
    )
```

```python
import functools
import jax
import jax.numpy as jnp
from jax import lax
from jax.experimental import pallas as pl
from jax.experimental.pallas import tpu as pltpu
from jax.sharding import PartitionSpec as P

HQ = 64
KVH = 8
HD = 128
PAGE = 8
STEPS = 2
KVD = 1024
GRP = HQ // KVH
MASKED = -1e30
VMEM = pltpu.MemorySpace.VMEM
SMEM = pltpu.MemorySpace.SMEM
LIMIT = 32 * 1024 * 1024


def whole(space):
    return pl.BlockSpec(memory_space=space)


def message_kernel(rows_p, rows_d, length, prefill_q, decode_q, owners, out, rows):
    for r in range(rows_p + rows_d):
        ref, at = (prefill_q, r) if r < rows_p else (decode_q, r - rows_p)
        line = ref[at : at + 1, :].astype(jnp.float32)
        for h in range(HQ):
            rows[r * HQ + h : r * HQ + h + 1, :] = line[:, h * HD : (h + 1) * HD]
    base = (rows_p + rows_d) * HQ
    slots = owners.shape[1]
    rows[base : base + 8, :] = jnp.zeros((8, 128), jnp.float32)
    rows[base : base + 1, 0:slots] = owners[...].astype(jnp.float32)
    lane = lax.broadcasted_iota(jnp.int32, (1, 128), 1)
    digits = jnp.zeros((1, 128), jnp.int32)
    for q in range(length.shape[1]):
        value = length[:, q : q + 1]
        digits = jnp.where(lane == 2 * q, value >> 8, digits)
        digits = jnp.where(lane == 2 * q + 1, value & 255, digits)
    rows[base + 1 : base + 2, :] = digits.astype(jnp.float32)
    out[...] = rows[...].reshape(out.shape).astype(jnp.bfloat16)


def make_message(prefill_q, decode_q, page_owner, context_len):
    rows_p = prefill_q.shape[0]
    rows_d = decode_q.shape[0] * STEPS
    blocks = (rows_p + rows_d) * KVH + 1
    return pl.pallas_call(
        functools.partial(message_kernel, rows_p, rows_d),
        out_shape=jax.ShapeDtypeStruct((blocks, 8, 128), jnp.bfloat16),
        in_specs=[whole(VMEM)] * 4,
        out_specs=whole(VMEM),
        scratch_shapes=[pltpu.VMEM((blocks * 8, 128), jnp.float32)],
        name="message",
    )(context_len.reshape(1, -1), prefill_q, decode_q.reshape(rows_d, HQ * HD), page_owner.reshape(1, -1))


def pack_kernel(shards, capacity, partners, owners, counts, keys, values, *refs):
    outs, (taken, chosen) = refs[:-2], refs[-2:]
    me = lax.axis_index("seq")

    def reset(o, carry):
        taken[o] = 0
        return carry

    lax.fori_loop(0, shards, reset, 0, unroll=8)

    def note(j, carry):
        o = owners[j]
        k = taken[o]
        taken[o] = k + 1
        chosen[o * capacity + k] = j
        return carry

    lax.fori_loop(0, counts[me], note, 0)
    for partner, out in zip(partners, outs):
        o = me ^ partner
        count = taken[o]

        def copy(k, carry, o=o, count=count, out=out):
            full = k < count
            j = jnp.where(full, chosen[o * capacity + k], 0)
            for part, pages in enumerate((keys, values)):
                page = pages[j]
                out[part, k] = jnp.where(full, page, jnp.zeros_like(page))
            return carry

        lax.fori_loop(0, capacity, copy, 0, unroll=2)


def pack(owners, counts, keys, values, shards, capacity, partners):
    slots = keys.shape[0]
    piece = jax.ShapeDtypeStruct((2, capacity, PAGE, KVD), keys.dtype)
    return pl.pallas_call(
        functools.partial(pack_kernel, shards, capacity, partners),
        out_shape=(piece,) * len(partners),
        in_specs=[whole(SMEM), whole(SMEM), whole(VMEM), whole(VMEM)],
        out_specs=(whole(VMEM),) * len(partners),
        scratch_shapes=[
            pltpu.SMEM((shards,), jnp.int32),
            pltpu.SMEM((shards * capacity,), jnp.int32),
        ],
        cost_estimate=pl.CostEstimate(
            flops=0,
            transcendentals=0,
            bytes_accessed=(2 * slots + 4 * len(partners) * capacity) * PAGE * KVD * 2,
        ),
        name="pack",
    )(owners, counts, keys, values)


def attend_kernel(rows_p, rows_d, capacity, counts, *refs):
    messages, refs = refs[:4], refs[4:]
    keys, values, keep, give, table, limits, stats, hits = refs
    me = lax.axis_index("seq")
    rows = rows_p + rows_d
    blocks = rows * KVH + 1
    shards = 4 * messages[0].shape[0] // blocks
    height = shards * rows * GRP
    held = keys.shape[0]

    def block(k, at):
        return messages[k % 4][(k // 4) * blocks + at]

    def count(d, carry):
        before, total = carry
        here = counts[d]
        return (before + jnp.where(d < me, here, 0), total + here)

    before, total = lax.fori_loop(0, shards, count, (jnp.int32(0), jnp.int32(0)))
    start = PAGE * before
    live = PAGE * counts[me]
    first = PAGE * total - shards * rows_p + 1
    lane = lax.broadcasted_iota(jnp.int32, (1, 128), 1)
    for k in range(shards):
        d = me ^ k
        tail = block(k, rows * KVH).astype(jnp.float32)
        for r in range(rows):
            at = (k * rows + r) * GRP
            if r < rows_p:
                bound = jnp.minimum(first + d * rows_p + r - start, live)
                limits[at : at + GRP, :] = jnp.full((GRP, 128), bound, jnp.int32)
            else:
                q = (r - rows_p) // STEPS
                length = tail[1:2, 2 * q : 2 * q + 1] * 256.0 + tail[1:2, 2 * q + 1 : 2 * q + 2]
                bound = jnp.minimum(length.astype(jnp.int32) - start, live)
                limits[at : at + GRP, :] = jnp.broadcast_to(bound, (GRP, 128))
        hit = (tail[0:1, :].astype(jnp.int32) == me) & (lane < counts[d])
        hits[pl.ds(d, 1), :] = hit.astype(jnp.float32)

    hit = hits[...]
    earlier = (
        lax.broadcasted_iota(jnp.int32, (128, 128), 0)
        < lax.broadcasted_iota(jnp.int32, (128, 128), 1)
    ).astype(jnp.bfloat16)
    rank = jnp.dot(hit.astype(jnp.bfloat16), earlier, preferred_element_type=jnp.float32)
    wide = lax.broadcasted_iota(jnp.int32, hit.shape, 1)
    depth = lax.broadcasted_iota(jnp.int32, hit.shape, 0)
    numbered = jnp.zeros(hit.shape, jnp.float32)
    for k in range(capacity):
        match = jnp.where((hit > 0.5) & (rank == float(k)), (wide + 1).astype(jnp.float32), 0.0)
        found = jnp.sum(match, axis=1, keepdims=True)
        numbered = jnp.where(wide == k, found, numbered)
    within = numbered.astype(jnp.int32)
    slots = held // PAGE
    table[...] = jnp.where(within > 0, depth * slots + within - 1, -1)

    stats[...] = jnp.zeros_like(stats)
    spot = lax.broadcasted_iota(jnp.int32, (height, 128), 1)
    column = lax.broadcasted_iota(jnp.int32, (height, held), 1)
    pieces = [(k, r, (k * rows + r) * GRP) for k in range(shards) for r in range(rows)]

    def target(k):
        return give if k % 2 else keep

    def one_group(g, carry):
        query = jnp.concatenate(
            [block(k, r * KVH + g).astype(jnp.float32) for k, r, _ in pieces], axis=0
        ).astype(jnp.bfloat16)
        across = pl.ds(pl.multiple_of(g * HD, HD), HD)
        scores = lax.dot_general(
            query, keys[:, across], (((1,), (1,)), ((), ())), preferred_element_type=jnp.float32
        ) * (HD ** (-0.5))
        allowed = column < jnp.concatenate([limits[...]] * (held // 128), axis=1)
        scores = jnp.where(allowed, scores, MASKED)
        high = jnp.max(scores, axis=1, keepdims=True).astype(jnp.bfloat16).astype(jnp.float32)
        weights = jnp.where(allowed, jnp.exp(scores - high), 0.0)
        total = jnp.sum(weights, axis=1, keepdims=True)
        product = jnp.dot(
            weights.astype(jnp.bfloat16), values[:, across], preferred_element_type=jnp.float32
        )
        coarse = total.astype(jnp.bfloat16).astype(jnp.float32)
        kept = jnp.where(spot == g, high, stats[...])
        kept = jnp.where(spot == KVH + g, coarse, kept)
        stats[...] = jnp.where(spot == 2 * KVH + g, total - coarse, kept)
        for k, r, at in pieces:
            target(k)[k // 2, r * KVH + g] = product[at : at + GRP, :].astype(jnp.bfloat16)
        return carry

    lax.fori_loop(0, KVH, one_group, 0)
    for k, r, at in pieces:
        target(k)[k // 2, rows * KVH + r] = stats[at : at + GRP, :].astype(jnp.bfloat16)


def attend(rows_p, rows_d, capacity, counts, messages, keys, values):
    rows = rows_p + rows_d
    shards = 4 * messages[0].shape[0] // (rows * KVH + 1)
    height = shards * rows * GRP
    held = keys.shape[0]
    half = jax.ShapeDtypeStruct((shards // 2, rows * (KVH + 1), GRP, 128), jnp.bfloat16)
    return pl.pallas_call(
        functools.partial(attend_kernel, rows_p, rows_d, capacity),
        out_shape=(half, half, jax.ShapeDtypeStruct((shards, 128), jnp.int32)),
        in_specs=[whole(SMEM)] + [whole(VMEM)] * 6,
        out_specs=(whole(VMEM),) * 3,
        scratch_shapes=[
            pltpu.VMEM((height, 128), jnp.int32),
            pltpu.VMEM((height, 128), jnp.float32),
            pltpu.VMEM((shards, 128), jnp.float32),
        ],
        compiler_params=pltpu.CompilerParams(vmem_limit_bytes=LIMIT),
        cost_estimate=pl.CostEstimate(
            flops=4 * height * KVH * held * HD,
            transcendentals=height * KVH * held,
            bytes_accessed=2 * held * KVD * 2 + 4 * height * KVH * HD,
        ),
        name="attend",
    )(counts, *messages, keys, values)


def fold_kernel(rows, keep, got, *outs):
    lane = lax.broadcasted_iota(jnp.int32, (GRP, 128), 1)
    inside = lane < KVH
    for j, out in enumerate(outs):
        for r in range(rows):
            raw = [ref[j, rows * KVH + r].astype(jnp.float32) for ref in (keep, got)]
            high = jnp.maximum(jnp.where(inside, raw[0], 0.0), jnp.where(inside, raw[1], 0.0))
            factors = [jnp.exp(jnp.where(inside, part, 0.0) - high) for part in raw]
            sizes = [
                pltpu.roll(part, 128 - KVH, 1) + pltpu.roll(part, 128 - 2 * KVH, 1) for part in raw
            ]
            total = jnp.where(inside, factors[0] * sizes[0] + factors[1] * sizes[1], 0.0)
            coarse = total.astype(jnp.bfloat16).astype(jnp.float32)
            line = high + pltpu.roll(coarse, KVH, 1) + pltpu.roll(total - coarse, 2 * KVH, 1)
            out[rows * KVH + r] = line.astype(jnp.bfloat16)
            for g in range(KVH):
                at = r * KVH + g
                mixed = factors[0][:, g : g + 1] * keep[j, at].astype(jnp.float32)
                mixed = mixed + factors[1][:, g : g + 1] * got[j, at].astype(jnp.float32)
                out[at] = mixed.astype(jnp.bfloat16)


def fold(rows, keep, got):
    piece = jax.ShapeDtypeStruct(keep.shape[1:], keep.dtype)
    return pl.pallas_call(
        functools.partial(fold_kernel, rows),
        out_shape=(piece,) * keep.shape[0],
        in_specs=[whole(VMEM)] * 2,
        out_specs=(whole(VMEM),) * keep.shape[0],
        compiler_params=pltpu.CompilerParams(vmem_limit_bytes=LIMIT),
        cost_estimate=pl.CostEstimate(
            flops=keep.size * 4, transcendentals=0, bytes_accessed=keep.size * 6
        ),
        name="fold",
    )(keep, got)


def settle_kernel(partners, old, *refs):
    refs = refs[old:]
    pieces, refs = refs[: len(partners)], refs[len(partners) :]
    store_k, store_v, held, sems_in, sems_out = refs
    me = lax.axis_index("seq")
    fetches = [
        pltpu.make_async_copy(piece, held.at[i], sems_in.at[i]) for i, piece in enumerate(pieces)
    ]
    for fetch in fetches:
        fetch.start()
    puts = []
    for i, (partner, fetch) in enumerate(zip(partners, fetches)):
        fetch.wait()
        for part, store in enumerate((store_k, store_v)):
            put = pltpu.make_async_copy(
                held.at[i, part], store.at[me ^ partner], sems_out.at[2 * i + part]
            )
            put.start()
            puts.append(put)
    for put in puts:
        put.wait()


def settle(shards, partners, pieces, stores=()):
    number = len(partners)
    shape = (shards,) + pieces[0].shape[1:]
    store = jax.ShapeDtypeStruct(shape, pieces[0].dtype)
    return pl.pallas_call(
        functools.partial(settle_kernel, partners, len(stores)),
        out_shape=(store, store),
        in_specs=[whole(pl.ANY)] * (len(stores) + number),
        out_specs=(whole(pl.ANY),) * 2,
        input_output_aliases={i: i for i in range(len(stores))},
        scratch_shapes=[
            pltpu.VMEM((number,) + pieces[0].shape, pieces[0].dtype),
            pltpu.SemaphoreType.DMA((number,)),
            pltpu.SemaphoreType.DMA((2 * number,)),
        ],
        cost_estimate=pl.CostEstimate(
            flops=0, transcendentals=0, bytes_accessed=4 * number * pieces[0].size
        ),
        name="settle",
    )(*stores, *pieces)


def merge_kernel(rows_p, rows_d, message, new_k, new_v, *refs):
    parts, (prefill_out, decode_out, lines) = refs[:-3], refs[-3:]
    sources = len(parts)
    rows = rows_p + rows_d
    lane = lax.broadcasted_iota(jnp.int32, (GRP, 128), 1)
    for r in range(rows):
        raw = [part[rows * KVH + r].astype(jnp.float32) for part in parts]
        high = functools.reduce(jnp.maximum, raw)
        fresh = []
        if r >= rows_p:
            request, step = divmod(r - rows_p, STEPS)
            for t in range(step + 1):
                score = jnp.zeros((GRP, 128), jnp.float32)
                for g in range(KVH):
                    query = message[r * KVH + g].astype(jnp.float32)
                    at = request * STEPS + t
                    key = new_k[at : at + 1, g * HD : (g + 1) * HD].astype(jnp.float32)
                    column = jnp.sum(query * key, axis=1, keepdims=True) * (HD ** (-0.5))
                    score = jnp.where(lane == g, column, score)
                fresh.append((request * STEPS + t, score))
                high = jnp.maximum(high, score)
        high = jnp.where(lane < KVH, high, 0.0)
        total = jnp.zeros((GRP, 128), jnp.float32)
        factors = []
        for s in range(sources):
            factor = jnp.exp(jnp.where(lane < KVH, raw[s], 0.0) - high)
            size = pltpu.roll(raw[s], 128 - KVH, 1) + pltpu.roll(raw[s], 128 - 2 * KVH, 1)
            total = total + factor * size
            factors.append(factor)
        fresh = [(at, jnp.exp(score - high)) for at, score in fresh]
        for _, weight in fresh:
            total = total + weight
        total = jnp.where(lane < KVH, total, 1.0)
        factors = [factor / total for factor in factors]
        fresh = [
            (at, (weight / total).astype(jnp.bfloat16).astype(jnp.float32)) for at, weight in fresh
        ]
        for g in range(KVH):
            result = jnp.zeros((GRP, HD), jnp.float32)
            for s in range(sources):
                block = parts[s][r * KVH + g].astype(jnp.float32)
                result = result + factors[s][:, g : g + 1] * block
            for at, weight in fresh:
                value = new_v[at : at + 1, g * HD : (g + 1) * HD].astype(jnp.float32)
                result = result + weight[:, g : g + 1] * value
            for h in range(GRP):
                column = (g * GRP + h) * HD
                lines[r : r + 1, column : column + HD] = result[h : h + 1, :]
    prefill_out[...] = lines[0:rows_p, :].astype(jnp.bfloat16)
    decode_out[...] = lines[rows_p:rows, :].astype(jnp.bfloat16)


def merge(rows_p, rows_d, parts, message, new_k, new_v):
    rows = rows_p + rows_d
    return pl.pallas_call(
        functools.partial(merge_kernel, rows_p, rows_d),
        out_shape=(
            jax.ShapeDtypeStruct((rows_p, HQ * HD), jnp.bfloat16),
            jax.ShapeDtypeStruct((rows_d, HQ * HD), jnp.bfloat16),
        ),
        in_specs=[whole(VMEM)] * (3 + len(parts)),
        out_specs=(whole(VMEM), whole(VMEM)),
        scratch_shapes=[pltpu.VMEM((rows, HQ * HD), jnp.float32)],
        compiler_params=pltpu.CompilerParams(vmem_limit_bytes=LIMIT),
        cost_estimate=pl.CostEstimate(
            flops=len(parts) * parts[0].size * 4,
            transcendentals=0,
            bytes_accessed=len(parts) * parts[0].size * 2,
        ),
        name="merge",
    )(message, new_k.reshape(rows_d, KVD), new_v.reshape(rows_d, KVD), *parts)


def swap(array, distance):
    shards = lax.axis_size("seq")
    return lax.ppermute(array, "seq", [(i, i ^ distance) for i in range(shards)])


def send_order(shards):
    upper = list(range(shards // 2, shards))
    lower = [k for k in range(1, shards // 2)]
    quarter = len(upper) // 2
    early = upper[:quarter]
    side = [k for k in lower if k >= 4] + [k for k in lower if k < 4]
    before, after = side[: quarter // 2], side[quarter // 2 :]
    late = upper[quarter:]
    return early, before, late, after


def per_device(
    prefill_q, cache_k, cache_v, page_counts, page_owner, decode_q, decode_k, decode_v, context_len
):
    shards = lax.axis_size("seq")
    page_slots = cache_k.shape[0] // PAGE
    capacity = max(2, 2 * page_slots // shards)
    rows_p = prefill_q.shape[0]
    rows_d = decode_q.shape[0] * STEPS
    owners = page_owner.reshape(-1)
    pages_k = cache_k.reshape(page_slots, PAGE, KVD)
    pages_v = cache_v.reshape(page_slots, PAGE, KVD)
    rows = rows_p + rows_d
    early, before, late, after = send_order(shards)
    pieces = {}
    message = make_message(prefill_q, decode_q, page_owner, context_len)
    far = [message]
    for k in range(4, shards, 4):
        far.append(swap(message, k))
    for group in (early, [0] + before + late + after):
        packed = pack(owners, page_counts, pages_k, pages_v, shards, capacity, group)
        for k, piece in zip(group, packed):
            pieces[k] = swap(piece, k) if k else piece
    own = jnp.concatenate(far, axis=0)
    across = swap(own, 2)
    beside = swap(own, 1)
    corner = swap(across, 1)
    keep, give, table = attend(
        rows_p,
        rows_d,
        capacity,
        page_counts,
        (own, beside, across, corner),
        cache_k,
        cache_v,
    )
    got = swap(give, 1)
    folded = fold(rows, keep, got)
    parts = [folded[0]]
    for j in range(1, shards // 2):
        parts.append(swap(folded[j], 2 * j))
    prefill_out, decode_out = merge(rows_p, rows_d, parts, message, decode_k, decode_v)
    stores = ()
    for group in ([0] + early + before, late[:-2] + after, late[-2:]):
        stores = settle(shards, group, [pieces[k] for k in group], stores)
    store_page = table[:, :capacity].reshape(-1)
    return (
        prefill_out,
        decode_out.reshape(decode_q.shape),
        stores[0].reshape(-1, KVD),
        stores[1].reshape(-1, KVD),
        store_page,
    )


def solution(mesh):
    in_specs = (
        P(("groups", "seq"), None),
        P(("groups", "seq"), None),
        P(("groups", "seq"), None),
        P("groups"),
        P(("groups", "seq"), None),
        P(("groups", "seq"), None, None),
        P(("groups", "seq"), None, None),
        P(("groups", "seq"), None, None),
        P(("groups", "seq")),
    )
    out_specs = (
        P(("groups", "seq"), None),
        P(("groups", "seq"), None, None),
        P(("groups", "seq"), None),
        P(("groups", "seq"), None),
        P(("groups", "seq")),
    )
    return jax.shard_map(
        per_device, mesh=mesh, in_specs=in_specs, out_specs=out_specs, check_vma=False
    )
```

```python
import functools
import jax
import jax.numpy as jnp
from jax import lax
from jax.experimental import pallas as pl
from jax.experimental.pallas import tpu as pltpu
from jax.sharding import PartitionSpec as P

HQ = 64
KVH = 8
HD = 128
PAGE = 8
STEPS = 2
KVD = 1024
GRP = HQ // KVH
MASKED = -1e30
VMEM = pltpu.MemorySpace.VMEM
SMEM = pltpu.MemorySpace.SMEM
LIMIT = 32 * 1024 * 1024
SMALL = 8 * 1024 * 1024


def whole(space):
    return pl.BlockSpec(memory_space=space)


def message_kernel(rows_p, rows_d, length, prefill_q, decode_q, owners, out, rows):
    for r in range(rows_p + rows_d):
        ref, at = (prefill_q, r) if r < rows_p else (decode_q, r - rows_p)
        line = ref[at : at + 1, :].astype(jnp.float32)
        for h in range(HQ):
            rows[r * HQ + h : r * HQ + h + 1, :] = line[:, h * HD : (h + 1) * HD]
    base = (rows_p + rows_d) * HQ
    slots = owners.shape[1]
    rows[base : base + 8, :] = jnp.zeros((8, 128), jnp.float32)
    rows[base : base + 1, 0:slots] = owners[...].astype(jnp.float32)
    lane = lax.broadcasted_iota(jnp.int32, (1, 128), 1)
    digits = jnp.zeros((1, 128), jnp.int32)
    for q in range(length.shape[1]):
        value = length[:, q : q + 1]
        digits = jnp.where(lane == 2 * q, value >> 8, digits)
        digits = jnp.where(lane == 2 * q + 1, value & 255, digits)
    rows[base + 1 : base + 2, :] = digits.astype(jnp.float32)
    out[...] = rows[...].reshape(out.shape).astype(jnp.bfloat16)


def make_message(prefill_q, decode_q, page_owner, context_len):
    rows_p = prefill_q.shape[0]
    rows_d = decode_q.shape[0] * STEPS
    blocks = (rows_p + rows_d) * KVH + 1
    return pl.pallas_call(
        functools.partial(message_kernel, rows_p, rows_d),
        out_shape=jax.ShapeDtypeStruct((blocks, 8, 128), jnp.bfloat16),
        in_specs=[whole(VMEM)] * 4,
        out_specs=whole(VMEM),
        scratch_shapes=[pltpu.VMEM((blocks * 8, 128), jnp.float32)],
        name="message",
    )(context_len.reshape(1, -1), prefill_q, decode_q.reshape(rows_d, HQ * HD), page_owner.reshape(1, -1))


def pack_kernel(shards, capacity, partners, owners, counts, keys, values, *refs):
    outs, (taken, chosen) = refs[:-2], refs[-2:]
    me = lax.axis_index("seq")

    def reset(o, carry):
        taken[o] = 0
        return carry

    lax.fori_loop(0, shards, reset, 0, unroll=8)

    def note(j, carry):
        o = owners[j]
        k = taken[o]
        taken[o] = k + 1
        chosen[o * capacity + k] = j
        return carry

    lax.fori_loop(0, counts[me], note, 0)
    for partner, out in zip(partners, outs):
        o = me ^ partner
        count = taken[o]

        def copy(k, carry, o=o, count=count, out=out):
            full = k < count
            j = jnp.where(full, chosen[o * capacity + k], 0)
            for part, pages in enumerate((keys, values)):
                page = pages[j]
                out[part, k] = jnp.where(full, page, jnp.zeros_like(page))
            return carry

        lax.fori_loop(0, capacity, copy, 0, unroll=2)


def pack(owners, counts, keys, values, shards, capacity, partners):
    slots = keys.shape[0]
    piece = jax.ShapeDtypeStruct((2, capacity, PAGE, KVD), keys.dtype)
    return pl.pallas_call(
        functools.partial(pack_kernel, shards, capacity, partners),
        out_shape=(piece,) * len(partners),
        in_specs=[whole(SMEM), whole(SMEM), whole(VMEM), whole(VMEM)],
        out_specs=(whole(VMEM),) * len(partners),
        scratch_shapes=[
            pltpu.SMEM((shards,), jnp.int32),
            pltpu.SMEM((shards * capacity,), jnp.int32),
        ],
        cost_estimate=pl.CostEstimate(
            flops=0,
            transcendentals=0,
            bytes_accessed=(2 * slots + 4 * len(partners) * capacity) * PAGE * KVD * 2,
        ),
        name="pack",
    )(owners, counts, keys, values)


def attend_kernel(rows_p, rows_d, capacity, counts, *refs):
    messages, refs = refs[:4], refs[4:]
    keys, values, keep, give, table, limits, stats, hits = refs
    me = lax.axis_index("seq")
    rows = rows_p + rows_d
    blocks = rows * KVH + 1
    shards = 4 * messages[0].shape[0] // blocks
    height = shards * rows * GRP
    held = keys.shape[0]

    def block(k, at):
        return messages[k % 4][(k // 4) * blocks + at]

    def count(d, carry):
        before, total = carry
        here = counts[d]
        return (before + jnp.where(d < me, here, 0), total + here)

    before, total = lax.fori_loop(0, shards, count, (jnp.int32(0), jnp.int32(0)))
    start = PAGE * before
    live = PAGE * counts[me]
    first = PAGE * total - shards * rows_p + 1
    lane = lax.broadcasted_iota(jnp.int32, (1, 128), 1)
    for k in range(shards):
        d = me ^ k
        tail = block(k, rows * KVH).astype(jnp.float32)
        for r in range(rows):
            at = (k * rows + r) * GRP
            if r < rows_p:
                bound = jnp.minimum(first + d * rows_p + r - start, live)
                limits[at : at + GRP, :] = jnp.full((GRP, 128), bound, jnp.int32)
            else:
                q = (r - rows_p) // STEPS
                length = tail[1:2, 2 * q : 2 * q + 1] * 256.0 + tail[1:2, 2 * q + 1 : 2 * q + 2]
                bound = jnp.minimum(length.astype(jnp.int32) - start, live)
                limits[at : at + GRP, :] = jnp.broadcast_to(bound, (GRP, 128))
        hit = (tail[0:1, :].astype(jnp.int32) == me) & (lane < counts[d])
        hits[pl.ds(d, 1), :] = hit.astype(jnp.float32)

    hit = hits[...]
    earlier = (
        lax.broadcasted_iota(jnp.int32, (128, 128), 0)
        < lax.broadcasted_iota(jnp.int32, (128, 128), 1)
    ).astype(jnp.bfloat16)
    rank = jnp.dot(hit.astype(jnp.bfloat16), earlier, preferred_element_type=jnp.float32)
    wide = lax.broadcasted_iota(jnp.int32, hit.shape, 1)
    depth = lax.broadcasted_iota(jnp.int32, hit.shape, 0)
    numbered = jnp.zeros(hit.shape, jnp.float32)
    for k in range(capacity):
        match = jnp.where((hit > 0.5) & (rank == float(k)), (wide + 1).astype(jnp.float32), 0.0)
        found = jnp.sum(match, axis=1, keepdims=True)
        numbered = jnp.where(wide == k, found, numbered)
    within = numbered.astype(jnp.int32)
    slots = held // PAGE
    table[...] = jnp.where(within > 0, depth * slots + within - 1, -1)

    stats[...] = jnp.zeros_like(stats)
    spot = lax.broadcasted_iota(jnp.int32, (height, 128), 1)
    column = lax.broadcasted_iota(jnp.int32, (height, held), 1)
    pieces = [(k, r, (k * rows + r) * GRP) for k in range(shards) for r in range(rows)]

    def target(k):
        return give if k % 2 else keep

    def one_group(g, carry):
        query = jnp.concatenate(
            [block(k, r * KVH + g).astype(jnp.float32) for k, r, _ in pieces], axis=0
        ).astype(jnp.bfloat16)
        across = pl.ds(pl.multiple_of(g * HD, HD), HD)
        scores = lax.dot_general(
            query, keys[:, across], (((1,), (1,)), ((), ())), preferred_element_type=jnp.float32
        ) * (HD ** (-0.5))
        allowed = column < jnp.concatenate([limits[...]] * (held // 128), axis=1)
        scores = jnp.where(allowed, scores, MASKED)
        high = jnp.max(scores, axis=1, keepdims=True).astype(jnp.bfloat16).astype(jnp.float32)
        weights = jnp.where(allowed, jnp.exp(scores - high), 0.0)
        total = jnp.sum(weights, axis=1, keepdims=True)
        product = jnp.dot(
            weights.astype(jnp.bfloat16), values[:, across], preferred_element_type=jnp.float32
        )
        coarse = total.astype(jnp.bfloat16).astype(jnp.float32)
        kept = jnp.where(spot == g, high, stats[...])
        kept = jnp.where(spot == KVH + g, coarse, kept)
        stats[...] = jnp.where(spot == 2 * KVH + g, total - coarse, kept)
        for k, r, at in pieces:
            target(k)[k // 2, r * KVH + g] = product[at : at + GRP, :].astype(jnp.bfloat16)
        return carry

    lax.fori_loop(0, KVH, one_group, 0)
    for k, r, at in pieces:
        target(k)[k // 2, rows * KVH + r] = stats[at : at + GRP, :].astype(jnp.bfloat16)


def attend(rows_p, rows_d, capacity, counts, messages, keys, values):
    rows = rows_p + rows_d
    shards = 4 * messages[0].shape[0] // (rows * KVH + 1)
    height = shards * rows * GRP
    held = keys.shape[0]
    half = jax.ShapeDtypeStruct((shards // 2, rows * (KVH + 1), GRP, 128), jnp.bfloat16)
    return pl.pallas_call(
        functools.partial(attend_kernel, rows_p, rows_d, capacity),
        out_shape=(half, half, jax.ShapeDtypeStruct((shards, 128), jnp.int32)),
        in_specs=[whole(SMEM)] + [whole(VMEM)] * 6,
        out_specs=(whole(VMEM),) * 3,
        scratch_shapes=[
            pltpu.VMEM((height, 128), jnp.int32),
            pltpu.VMEM((height, 128), jnp.float32),
            pltpu.VMEM((shards, 128), jnp.float32),
        ],
        compiler_params=pltpu.CompilerParams(vmem_limit_bytes=LIMIT),
        cost_estimate=pl.CostEstimate(
            flops=4 * height * KVH * held * HD,
            transcendentals=height * KVH * held,
            bytes_accessed=2 * held * KVD * 2 + 4 * height * KVH * HD,
        ),
        name="attend",
    )(counts, *messages, keys, values)


def fold_kernel(rows, split, keep, got, *outs):
    lane = lax.broadcasted_iota(jnp.int32, (GRP, 128), 1)
    inside = lane < KVH

    def put(j, at, value):
        value = value.astype(jnp.bfloat16)
        if split:
            outs[j % 2][j // 2, at] = value
        else:
            outs[j][at] = value

    for j in range(keep.shape[0]):
        for r in range(rows):
            raw = [ref[j, rows * KVH + r].astype(jnp.float32) for ref in (keep, got)]
            high = jnp.maximum(jnp.where(inside, raw[0], 0.0), jnp.where(inside, raw[1], 0.0))
            factors = [jnp.exp(jnp.where(inside, part, 0.0) - high) for part in raw]
            sizes = [
                pltpu.roll(part, 128 - KVH, 1) + pltpu.roll(part, 128 - 2 * KVH, 1) for part in raw
            ]
            total = jnp.where(inside, factors[0] * sizes[0] + factors[1] * sizes[1], 0.0)
            coarse = total.astype(jnp.bfloat16).astype(jnp.float32)
            line = high + pltpu.roll(coarse, KVH, 1) + pltpu.roll(total - coarse, 2 * KVH, 1)
            put(j, rows * KVH + r, line)
            for g in range(KVH):
                at = r * KVH + g
                mixed = factors[0][:, g : g + 1] * keep[j, at].astype(jnp.float32)
                mixed = mixed + factors[1][:, g : g + 1] * got[j, at].astype(jnp.float32)
                put(j, at, mixed)


def fold(rows, split, keep, got):
    number = keep.shape[0]
    if split:
        half = jax.ShapeDtypeStruct((number // 2,) + keep.shape[1:], keep.dtype)
        outs = (half, half)
    else:
        outs = (jax.ShapeDtypeStruct(keep.shape[1:], keep.dtype),) * number
    return pl.pallas_call(
        functools.partial(fold_kernel, rows, split),
        out_shape=outs,
        in_specs=[whole(VMEM)] * 2,
        out_specs=(whole(VMEM),) * len(outs),
        compiler_params=pltpu.CompilerParams(vmem_limit_bytes=LIMIT),
        cost_estimate=pl.CostEstimate(
            flops=keep.size * 4, transcendentals=0, bytes_accessed=keep.size * 6
        ),
        name="fold",
    )(keep, got)


def settle_kernel(partners, old, *refs):
    refs = refs[old:]
    pieces, (store_k, store_v, sems) = refs[: len(partners)], refs[len(partners) :]
    me = lax.axis_index("seq")
    puts = []
    for partner, piece in zip(partners, pieces):
        for part, store in enumerate((store_k, store_v)):
            puts.append(
                pltpu.make_async_copy(
                    piece.at[part], store.at[me ^ partner], sems.at[len(puts)]
                )
            )
    for put in puts:
        put.start()
    for put in puts:
        put.wait()


def settle(shards, partners, pieces, stores):
    number = len(partners)
    shape = (shards,) + pieces[0].shape[1:]
    store = jax.ShapeDtypeStruct(shape, pieces[0].dtype)
    return pl.pallas_call(
        functools.partial(settle_kernel, partners, len(stores)),
        out_shape=(store, store),
        in_specs=[whole(pl.ANY)] * len(stores) + [whole(VMEM)] * number,
        out_specs=(whole(pl.ANY),) * 2,
        input_output_aliases={i: i for i in range(len(stores))},
        scratch_shapes=[pltpu.SemaphoreType.DMA((2 * number,))],
        compiler_params=pltpu.CompilerParams(vmem_limit_bytes=SMALL),
        cost_estimate=pl.CostEstimate(
            flops=0, transcendentals=0, bytes_accessed=4 * number * pieces[0].size
        ),
        name="settle",
    )(*stores, *pieces)


def merge_kernel(rows_p, rows_d, message, new_k, new_v, *refs):
    parts, (prefill_out, decode_out, lines) = refs[:-3], refs[-3:]
    sources = len(parts)
    rows = rows_p + rows_d
    lane = lax.broadcasted_iota(jnp.int32, (GRP, 128), 1)
    for r in range(rows):
        raw = [part[rows * KVH + r].astype(jnp.float32) for part in parts]
        high = functools.reduce(jnp.maximum, raw)
        fresh = []
        if r >= rows_p:
            request, step = divmod(r - rows_p, STEPS)
            for t in range(step + 1):
                score = jnp.zeros((GRP, 128), jnp.float32)
                for g in range(KVH):
                    query = message[r * KVH + g].astype(jnp.float32)
                    at = request * STEPS + t
                    key = new_k[at : at + 1, g * HD : (g + 1) * HD].astype(jnp.float32)
                    column = jnp.sum(query * key, axis=1, keepdims=True) * (HD ** (-0.5))
                    score = jnp.where(lane == g, column, score)
                fresh.append((request * STEPS + t, score))
                high = jnp.maximum(high, score)
        high = jnp.where(lane < KVH, high, 0.0)
        total = jnp.zeros((GRP, 128), jnp.float32)
        factors = []
        for s in range(sources):
            factor = jnp.exp(jnp.where(lane < KVH, raw[s], 0.0) - high)
            size = pltpu.roll(raw[s], 128 - KVH, 1) + pltpu.roll(raw[s], 128 - 2 * KVH, 1)
            total = total + factor * size
            factors.append(factor)
        fresh = [(at, jnp.exp(score - high)) for at, score in fresh]
        for _, weight in fresh:
            total = total + weight
        total = jnp.where(lane < KVH, total, 1.0)
        factors = [factor / total for factor in factors]
        fresh = [
            (at, (weight / total).astype(jnp.bfloat16).astype(jnp.float32)) for at, weight in fresh
        ]
        for g in range(KVH):
            result = jnp.zeros((GRP, HD), jnp.float32)
            for s in range(sources):
                block = parts[s][r * KVH + g].astype(jnp.float32)
                result = result + factors[s][:, g : g + 1] * block
            for at, weight in fresh:
                value = new_v[at : at + 1, g * HD : (g + 1) * HD].astype(jnp.float32)
                result = result + weight[:, g : g + 1] * value
            for h in range(GRP):
                column = (g * GRP + h) * HD
                lines[r : r + 1, column : column + HD] = result[h : h + 1, :]
    prefill_out[...] = lines[0:rows_p, :].astype(jnp.bfloat16)
    decode_out[...] = lines[rows_p:rows, :].astype(jnp.bfloat16)


def merge(rows_p, rows_d, parts, message, new_k, new_v):
    rows = rows_p + rows_d
    return pl.pallas_call(
        functools.partial(merge_kernel, rows_p, rows_d),
        out_shape=(
            jax.ShapeDtypeStruct((rows_p, HQ * HD), jnp.bfloat16),
            jax.ShapeDtypeStruct((rows_d, HQ * HD), jnp.bfloat16),
        ),
        in_specs=[whole(VMEM)] * (3 + len(parts)),
        out_specs=(whole(VMEM), whole(VMEM)),
        scratch_shapes=[pltpu.VMEM((rows, HQ * HD), jnp.float32)],
        compiler_params=pltpu.CompilerParams(vmem_limit_bytes=LIMIT),
        cost_estimate=pl.CostEstimate(
            flops=len(parts) * parts[0].size * 4,
            transcendentals=0,
            bytes_accessed=len(parts) * parts[0].size * 2,
        ),
        name="merge",
    )(message, new_k.reshape(rows_d, KVD), new_v.reshape(rows_d, KVD), *parts)


def swap(array, distance):
    shards = lax.axis_size("seq")
    return lax.ppermute(array, "seq", [(i, i ^ distance) for i in range(shards)])


def send_order(shards):
    upper = list(range(shards // 2, shards))
    side = [k for k in range(1, shards // 2) if k >= 4] + [1, 2, 3]
    half = len(upper) // 2
    first = upper[:1]
    second = upper[1:half] + side[:2] + upper[half : half + 1] + side[2:3]
    third = upper[half + 1 : half + 2] + side[3:]
    fourth = upper[half + 2 :]
    return first, second, third, fourth


def per_device(
    prefill_q, cache_k, cache_v, page_counts, page_owner, decode_q, decode_k, decode_v, context_len
):
    shards = lax.axis_size("seq")
    page_slots = cache_k.shape[0] // PAGE
    capacity = max(2, 2 * page_slots // shards)
    rows_p = prefill_q.shape[0]
    rows_d = decode_q.shape[0] * STEPS
    owners = page_owner.reshape(-1)
    pages_k = cache_k.reshape(page_slots, PAGE, KVD)
    pages_v = cache_v.reshape(page_slots, PAGE, KVD)
    rows = rows_p + rows_d
    first, second, third, fourth = send_order(shards)
    pieces = {}
    message = make_message(prefill_q, decode_q, page_owner, context_len)
    far = [message]
    for k in range(4, shards, 4):
        far.append(swap(message, k))
    for group in (first, [0] + second + third + fourth):
        packed = pack(owners, page_counts, pages_k, pages_v, shards, capacity, group)
        for k, piece in zip(group, packed):
            pieces[k] = swap(piece, k) if k else piece
    own = jnp.concatenate(far, axis=0)
    across = swap(own, 2)
    beside = swap(own, 1)
    corner = swap(across, 1)
    keep, give, table = attend(
        rows_p,
        rows_d,
        capacity,
        page_counts,
        (own, beside, across, corner),
        cache_k,
        cache_v,
    )
    got = swap(give, 1)
    keep, give = fold(rows, True, keep, got)
    got = swap(give, 2)
    folded = fold(rows, False, keep, got)
    parts = [folded[0]]
    for j in range(1, shards // 4):
        parts.append(swap(folded[j], 4 * j))
    prefill_out, decode_out = merge(rows_p, rows_d, parts, message, decode_k, decode_v)
    stores = ()
    for group in ([0] + first + second, third, fourth):
        stores = settle(shards, group, [pieces[k] for k in group], stores)
    store_page = table[:, :capacity].reshape(-1)
    return (
        prefill_out,
        decode_out.reshape(decode_q.shape),
        stores[0].reshape(-1, KVD),
        stores[1].reshape(-1, KVD),
        store_page,
    )


def solution(mesh):
    in_specs = (
        P(("groups", "seq"), None),
        P(("groups", "seq"), None),
        P(("groups", "seq"), None),
        P("groups"),
        P(("groups", "seq"), None),
        P(("groups", "seq"), None, None),
        P(("groups", "seq"), None, None),
        P(("groups", "seq"), None, None),
        P(("groups", "seq")),
    )
    out_specs = (
        P(("groups", "seq"), None),
        P(("groups", "seq"), None, None),
        P(("groups", "seq"), None),
        P(("groups", "seq"), None),
        P(("groups", "seq")),
    )
    return jax.shard_map(
        per_device, mesh=mesh, in_specs=in_specs, out_specs=out_specs, check_vma=False
    )
```

```python
import functools
import jax
import jax.numpy as jnp
from jax import lax
from jax.experimental import pallas as pl
from jax.experimental.pallas import tpu as pltpu
from jax.sharding import PartitionSpec as P

HQ = 64
KVH = 8
HD = 128
PAGE = 8
STEPS = 2
KVD = 1024
GRP = HQ // KVH
MASKED = -1e30
VMEM = pltpu.MemorySpace.VMEM
SMEM = pltpu.MemorySpace.SMEM
LIMIT = 32 * 1024 * 1024
SMALL = 8 * 1024 * 1024


def whole(space):
    return pl.BlockSpec(memory_space=space)


def message_kernel(rows_p, rows_d, length, prefill_q, decode_q, owners, out, rows):
    for r in range(rows_p + rows_d):
        ref, at = (prefill_q, r) if r < rows_p else (decode_q, r - rows_p)
        line = ref[at : at + 1, :].astype(jnp.float32)
        for h in range(HQ):
            rows[r * HQ + h : r * HQ + h + 1, :] = line[:, h * HD : (h + 1) * HD]
    base = (rows_p + rows_d) * HQ
    slots = owners.shape[1]
    rows[base : base + 8, :] = jnp.zeros((8, 128), jnp.float32)
    rows[base : base + 1, 0:slots] = owners[...].astype(jnp.float32)
    lane = lax.broadcasted_iota(jnp.int32, (1, 128), 1)
    digits = jnp.zeros((1, 128), jnp.int32)
    for q in range(length.shape[1]):
        value = length[:, q : q + 1]
        digits = jnp.where(lane == 2 * q, value >> 8, digits)
        digits = jnp.where(lane == 2 * q + 1, value & 255, digits)
    rows[base + 1 : base + 2, :] = digits.astype(jnp.float32)
    out[...] = rows[...].reshape(out.shape).astype(jnp.bfloat16)


def make_message(prefill_q, decode_q, page_owner, context_len):
    rows_p = prefill_q.shape[0]
    rows_d = decode_q.shape[0] * STEPS
    blocks = (rows_p + rows_d) * KVH + 1
    return pl.pallas_call(
        functools.partial(message_kernel, rows_p, rows_d),
        out_shape=jax.ShapeDtypeStruct((blocks, 8, 128), jnp.bfloat16),
        in_specs=[whole(VMEM)] * 4,
        out_specs=whole(VMEM),
        scratch_shapes=[pltpu.VMEM((blocks * 8, 128), jnp.float32)],
        name="message",
    )(context_len.reshape(1, -1), prefill_q, decode_q.reshape(rows_d, HQ * HD), page_owner.reshape(1, -1))


def pack_kernel(shards, capacity, partners, owners, counts, keys, values, *refs):
    outs, (taken, chosen) = refs[:-2], refs[-2:]
    me = lax.axis_index("seq")

    def reset(o, carry):
        taken[o] = 0
        return carry

    lax.fori_loop(0, shards, reset, 0, unroll=8)

    def note(j, carry):
        o = owners[j]
        k = taken[o]
        taken[o] = k + 1
        chosen[o * capacity + k] = j
        return carry

    lax.fori_loop(0, counts[me], note, 0)
    for partner, out in zip(partners, outs):
        o = me ^ partner
        count = taken[o]

        def copy(k, carry, o=o, count=count, out=out):
            full = k < count
            j = jnp.where(full, chosen[o * capacity + k], 0)
            for part, pages in enumerate((keys, values)):
                page = pages[j]
                out[part, k] = jnp.where(full, page, jnp.zeros_like(page))
            return carry

        lax.fori_loop(0, capacity, copy, 0, unroll=2)


def pack(owners, counts, keys, values, shards, capacity, partners):
    slots = keys.shape[0]
    piece = jax.ShapeDtypeStruct((2, capacity, PAGE, KVD), keys.dtype)
    return pl.pallas_call(
        functools.partial(pack_kernel, shards, capacity, partners),
        out_shape=(piece,) * len(partners),
        in_specs=[whole(SMEM), whole(SMEM), whole(VMEM), whole(VMEM)],
        out_specs=(whole(VMEM),) * len(partners),
        scratch_shapes=[
            pltpu.SMEM((shards,), jnp.int32),
            pltpu.SMEM((shards * capacity,), jnp.int32),
        ],
        cost_estimate=pl.CostEstimate(
            flops=0,
            transcendentals=0,
            bytes_accessed=(2 * slots + 4 * len(partners) * capacity) * PAGE * KVD * 2,
        ),
        name="pack",
    )(owners, counts, keys, values)


def pick_kernel(capacity, partner, owners, counts, keys, values, out, sem):
    me = lax.axis_index("seq")
    wanted = me ^ partner

    def fetch(j, k, start):
        for part, pages in enumerate((keys, values)):
            copy = pltpu.make_async_copy(pages.at[j], out.at[part, k], sem)
            if start:
                copy.start()
            else:
                copy.wait()

    def look(j, k):
        match = owners[j] == wanted

        @pl.when(match)
        def _():
            fetch(j, k, True)

        return k + match.astype(jnp.int32)

    found = lax.fori_loop(0, counts[me], look, jnp.int32(0))
    blank = jnp.zeros(out.shape[2:], out.dtype)

    def clear(k, carry):
        for part in range(2):
            out[part, k] = blank
        return carry

    lax.fori_loop(found, capacity, clear, 0)

    def arrive(k, carry):
        fetch(0, k, False)
        return carry

    lax.fori_loop(0, found, arrive, 0)


def pick(owners, counts, keys, values, capacity, partner):
    return pl.pallas_call(
        functools.partial(pick_kernel, capacity, partner),
        out_shape=jax.ShapeDtypeStruct((2, capacity, PAGE, KVD), keys.dtype),
        in_specs=[whole(SMEM), whole(SMEM), whole(pl.ANY), whole(pl.ANY)],
        out_specs=whole(VMEM),
        scratch_shapes=[pltpu.SemaphoreType.DMA],
        cost_estimate=pl.CostEstimate(
            flops=0, transcendentals=0, bytes_accessed=8 * capacity * PAGE * KVD
        ),
        name="pick",
    )(owners, counts, keys, values)


def attend_kernel(rows_p, rows_d, capacity, counts, *refs):
    messages, refs = refs[:4], refs[4:]
    keys, values, keep, give, table, limits, stats, hits = refs
    me = lax.axis_index("seq")
    rows = rows_p + rows_d
    blocks = rows * KVH + 1
    shards = 4 * messages[0].shape[0] // blocks
    height = shards * rows * GRP
    held = keys.shape[0]

    def block(k, at):
        return messages[k % 4][(k // 4) * blocks + at]

    def count(d, carry):
        before, total = carry
        here = counts[d]
        return (before + jnp.where(d < me, here, 0), total + here)

    before, total = lax.fori_loop(0, shards, count, (jnp.int32(0), jnp.int32(0)))
    start = PAGE * before
    live = PAGE * counts[me]
    first = PAGE * total - shards * rows_p + 1
    lane = lax.broadcasted_iota(jnp.int32, (1, 128), 1)
    for k in range(shards):
        d = me ^ k
        tail = block(k, rows * KVH).astype(jnp.float32)
        for r in range(rows):
            at = (k * rows + r) * GRP
            if r < rows_p:
                bound = jnp.minimum(first + d * rows_p + r - start, live)
                limits[at : at + GRP, :] = jnp.full((GRP, 128), bound, jnp.int32)
            else:
                q = (r - rows_p) // STEPS
                length = tail[1:2, 2 * q : 2 * q + 1] * 256.0 + tail[1:2, 2 * q + 1 : 2 * q + 2]
                bound = jnp.minimum(length.astype(jnp.int32) - start, live)
                limits[at : at + GRP, :] = jnp.broadcast_to(bound, (GRP, 128))
        hit = (tail[0:1, :].astype(jnp.int32) == me) & (lane < counts[d])
        hits[pl.ds(d, 1), :] = hit.astype(jnp.float32)

    hit = hits[...]
    earlier = (
        lax.broadcasted_iota(jnp.int32, (128, 128), 0)
        < lax.broadcasted_iota(jnp.int32, (128, 128), 1)
    ).astype(jnp.bfloat16)
    rank = jnp.dot(hit.astype(jnp.bfloat16), earlier, preferred_element_type=jnp.float32)
    wide = lax.broadcasted_iota(jnp.int32, hit.shape, 1)
    depth = lax.broadcasted_iota(jnp.int32, hit.shape, 0)
    numbered = jnp.zeros(hit.shape, jnp.float32)
    for k in range(capacity):
        match = jnp.where((hit > 0.5) & (rank == float(k)), (wide + 1).astype(jnp.float32), 0.0)
        found = jnp.sum(match, axis=1, keepdims=True)
        numbered = jnp.where(wide == k, found, numbered)
    within = numbered.astype(jnp.int32)
    slots = held // PAGE
    table[...] = jnp.where(within > 0, depth * slots + within - 1, -1)

    stats[...] = jnp.zeros_like(stats)
    spot = lax.broadcasted_iota(jnp.int32, (height, 128), 1)
    column = lax.broadcasted_iota(jnp.int32, (height, held), 1)
    pieces = [(k, r, (k * rows + r) * GRP) for k in range(shards) for r in range(rows)]

    def target(k):
        return give if k % 2 else keep

    def one_group(g, carry):
        query = jnp.concatenate(
            [block(k, r * KVH + g).astype(jnp.float32) for k, r, _ in pieces], axis=0
        ).astype(jnp.bfloat16)
        across = pl.ds(pl.multiple_of(g * HD, HD), HD)
        scores = lax.dot_general(
            query, keys[:, across], (((1,), (1,)), ((), ())), preferred_element_type=jnp.float32
        ) * (HD ** (-0.5))
        allowed = column < jnp.concatenate([limits[...]] * (held // 128), axis=1)
        scores = jnp.where(allowed, scores, MASKED)
        high = jnp.max(scores, axis=1, keepdims=True).astype(jnp.bfloat16).astype(jnp.float32)
        weights = jnp.where(allowed, jnp.exp(scores - high), 0.0)
        total = jnp.sum(weights, axis=1, keepdims=True)
        product = jnp.dot(
            weights.astype(jnp.bfloat16), values[:, across], preferred_element_type=jnp.float32
        )
        coarse = total.astype(jnp.bfloat16).astype(jnp.float32)
        kept = jnp.where(spot == g, high, stats[...])
        kept = jnp.where(spot == KVH + g, coarse, kept)
        stats[...] = jnp.where(spot == 2 * KVH + g, total - coarse, kept)
        for k, r, at in pieces:
            target(k)[k // 2, r * KVH + g] = product[at : at + GRP, :].astype(jnp.bfloat16)
        return carry

    lax.fori_loop(0, KVH, one_group, 0)
    for k, r, at in pieces:
        target(k)[k // 2, rows * KVH + r] = stats[at : at + GRP, :].astype(jnp.bfloat16)


def attend(rows_p, rows_d, capacity, counts, messages, keys, values):
    rows = rows_p + rows_d
    shards = 4 * messages[0].shape[0] // (rows * KVH + 1)
    height = shards * rows * GRP
    held = keys.shape[0]
    half = jax.ShapeDtypeStruct((shards // 2, rows * (KVH + 1), GRP, 128), jnp.bfloat16)
    return pl.pallas_call(
        functools.partial(attend_kernel, rows_p, rows_d, capacity),
        out_shape=(half, half, jax.ShapeDtypeStruct((shards, 128), jnp.int32)),
        in_specs=[whole(SMEM)] + [whole(VMEM)] * 6,
        out_specs=(whole(VMEM),) * 3,
        scratch_shapes=[
            pltpu.VMEM((height, 128), jnp.int32),
            pltpu.VMEM((height, 128), jnp.float32),
            pltpu.VMEM((shards, 128), jnp.float32),
        ],
        compiler_params=pltpu.CompilerParams(vmem_limit_bytes=LIMIT),
        cost_estimate=pl.CostEstimate(
            flops=4 * height * KVH * held * HD,
            transcendentals=height * KVH * held,
            bytes_accessed=2 * held * KVD * 2 + 4 * height * KVH * HD,
        ),
        name="attend",
    )(counts, *messages, keys, values)


def fold_kernel(rows, keep, got, *outs):
    lane = lax.broadcasted_iota(jnp.int32, (GRP, 128), 1)
    inside = lane < KVH

    def put(j, at, value):
        outs[j % 2][j // 2, at] = value.astype(jnp.bfloat16)

    for j in range(keep.shape[0]):
        for r in range(rows):
            raw = [ref[j, rows * KVH + r].astype(jnp.float32) for ref in (keep, got)]
            high = jnp.maximum(jnp.where(inside, raw[0], 0.0), jnp.where(inside, raw[1], 0.0))
            factors = [jnp.exp(jnp.where(inside, part, 0.0) - high) for part in raw]
            sizes = [
                pltpu.roll(part, 128 - KVH, 1) + pltpu.roll(part, 128 - 2 * KVH, 1) for part in raw
            ]
            total = jnp.where(inside, factors[0] * sizes[0] + factors[1] * sizes[1], 0.0)
            coarse = total.astype(jnp.bfloat16).astype(jnp.float32)
            line = high + pltpu.roll(coarse, KVH, 1) + pltpu.roll(total - coarse, 2 * KVH, 1)
            put(j, rows * KVH + r, line)
            for g in range(KVH):
                at = r * KVH + g
                mixed = factors[0][:, g : g + 1] * keep[j, at].astype(jnp.float32)
                mixed = mixed + factors[1][:, g : g + 1] * got[j, at].astype(jnp.float32)
                put(j, at, mixed)


def fold(rows, keep, got):
    half = jax.ShapeDtypeStruct((keep.shape[0] // 2,) + keep.shape[1:], keep.dtype)
    return pl.pallas_call(
        functools.partial(fold_kernel, rows),
        out_shape=(half, half),
        in_specs=[whole(VMEM)] * 2,
        out_specs=(whole(VMEM),) * 2,
        compiler_params=pltpu.CompilerParams(vmem_limit_bytes=LIMIT),
        cost_estimate=pl.CostEstimate(
            flops=keep.size * 4, transcendentals=0, bytes_accessed=keep.size * 6
        ),
        name="fold",
    )(keep, got)


def settle_kernel(partners, old, *refs):
    refs = refs[old:]
    pieces, (store_k, store_v, sems) = refs[: len(partners)], refs[len(partners) :]
    me = lax.axis_index("seq")
    puts = []
    for partner, piece in zip(partners, pieces):
        for part, store in enumerate((store_k, store_v)):
            puts.append(
                pltpu.make_async_copy(
                    piece.at[part], store.at[me ^ partner], sems.at[len(puts)]
                )
            )
    for put in puts:
        put.start()
    for put in puts:
        put.wait()


def settle(shards, partners, pieces, stores):
    number = len(partners)
    shape = (shards,) + pieces[0].shape[1:]
    store = jax.ShapeDtypeStruct(shape, pieces[0].dtype)
    return pl.pallas_call(
        functools.partial(settle_kernel, partners, len(stores)),
        out_shape=(store, store),
        in_specs=[whole(pl.ANY)] * len(stores) + [whole(VMEM)] * number,
        out_specs=(whole(pl.ANY),) * 2,
        input_output_aliases={i: i for i in range(len(stores))},
        scratch_shapes=[pltpu.SemaphoreType.DMA((2 * number,))],
        compiler_params=pltpu.CompilerParams(vmem_limit_bytes=SMALL),
        cost_estimate=pl.CostEstimate(
            flops=0, transcendentals=0, bytes_accessed=4 * number * pieces[0].size
        ),
        name="settle",
    )(*stores, *pieces)


def merge_kernel(rows_p, rows_d, message, new_k, new_v, *refs):
    parts, (prefill_out, decode_out, lines) = refs[:-3], refs[-3:]
    sources = len(parts)
    rows = rows_p + rows_d
    lane = lax.broadcasted_iota(jnp.int32, (GRP, 128), 1)
    for r in range(rows):
        raw = [part[0, rows * KVH + r].astype(jnp.float32) for part in parts]
        high = functools.reduce(jnp.maximum, raw)
        fresh = []
        if r >= rows_p:
            request, step = divmod(r - rows_p, STEPS)
            for t in range(step + 1):
                score = jnp.zeros((GRP, 128), jnp.float32)
                for g in range(KVH):
                    query = message[r * KVH + g].astype(jnp.float32)
                    at = request * STEPS + t
                    key = new_k[at : at + 1, g * HD : (g + 1) * HD].astype(jnp.float32)
                    column = jnp.sum(query * key, axis=1, keepdims=True) * (HD ** (-0.5))
                    score = jnp.where(lane == g, column, score)
                fresh.append((request * STEPS + t, score))
                high = jnp.maximum(high, score)
        high = jnp.where(lane < KVH, high, 0.0)
        total = jnp.zeros((GRP, 128), jnp.float32)
        factors = []
        for s in range(sources):
            factor = jnp.exp(jnp.where(lane < KVH, raw[s], 0.0) - high)
            size = pltpu.roll(raw[s], 128 - KVH, 1) + pltpu.roll(raw[s], 128 - 2 * KVH, 1)
            total = total + factor * size
            factors.append(factor)
        fresh = [(at, jnp.exp(score - high)) for at, score in fresh]
        for _, weight in fresh:
            total = total + weight
        total = jnp.where(lane < KVH, total, 1.0)
        factors = [factor / total for factor in factors]
        fresh = [
            (at, (weight / total).astype(jnp.bfloat16).astype(jnp.float32)) for at, weight in fresh
        ]
        for g in range(KVH):
            result = jnp.zeros((GRP, HD), jnp.float32)
            for s in range(sources):
                block = parts[s][0, r * KVH + g].astype(jnp.float32)
                result = result + factors[s][:, g : g + 1] * block
            for at, weight in fresh:
                value = new_v[at : at + 1, g * HD : (g + 1) * HD].astype(jnp.float32)
                result = result + weight[:, g : g + 1] * value
            for h in range(GRP):
                column = (g * GRP + h) * HD
                lines[r : r + 1, column : column + HD] = result[h : h + 1, :]
    prefill_out[...] = lines[0:rows_p, :].astype(jnp.bfloat16)
    decode_out[...] = lines[rows_p:rows, :].astype(jnp.bfloat16)


def merge(rows_p, rows_d, parts, message, new_k, new_v):
    rows = rows_p + rows_d
    return pl.pallas_call(
        functools.partial(merge_kernel, rows_p, rows_d),
        out_shape=(
            jax.ShapeDtypeStruct((rows_p, HQ * HD), jnp.bfloat16),
            jax.ShapeDtypeStruct((rows_d, HQ * HD), jnp.bfloat16),
        ),
        in_specs=[whole(VMEM)] * (3 + len(parts)),
        out_specs=(whole(VMEM), whole(VMEM)),
        scratch_shapes=[pltpu.VMEM((rows, HQ * HD), jnp.float32)],
        compiler_params=pltpu.CompilerParams(vmem_limit_bytes=LIMIT),
        cost_estimate=pl.CostEstimate(
            flops=len(parts) * parts[0].size * 4,
            transcendentals=0,
            bytes_accessed=len(parts) * parts[0].size * 2,
        ),
        name="merge",
    )(message, new_k.reshape(rows_d, KVD), new_v.reshape(rows_d, KVD), *parts)


def swap(array, distance):
    shards = lax.axis_size("seq")
    return lax.ppermute(array, "seq", [(i, i ^ distance) for i in range(shards)])


def send_order(shards):
    upper = range(shards // 2, shards)
    side = range(4, shards // 2)
    plain, plain_side = [[k for k in group if not k & 2] for group in (upper, side)]
    other, other_side = [[k for k in group if k & 2] for group in (upper, side)]
    half = len(other) // 2
    first = plain[0]
    opening = plain[1:2] + plain_side[: len(plain_side) // 2] + plain[2:3]
    second = plain_side[len(plain_side) // 2 :] + plain[3:]
    third = other[:half] + other_side
    return first, opening, second, third, [1, 2, 3], other[half:]


def bits_of(shards):
    return [1 << b for b in range(shards.bit_length() - 1)]


def per_device(
    prefill_q, cache_k, cache_v, page_counts, page_owner, decode_q, decode_k, decode_v, context_len
):
    shards = lax.axis_size("seq")
    page_slots = cache_k.shape[0] // PAGE
    capacity = max(2, 2 * page_slots // shards)
    rows_p = prefill_q.shape[0]
    rows_d = decode_q.shape[0] * STEPS
    owners = page_owner.reshape(-1)
    pages_k = cache_k.reshape(page_slots, PAGE, KVD)
    pages_v = cache_v.reshape(page_slots, PAGE, KVD)
    rows = rows_p + rows_d
    first, opening, second, third, near, last = send_order(shards)
    piece = pick(owners, page_counts, pages_k, pages_v, capacity, first)
    pieces = {first: swap(piece, first)}
    message = make_message(prefill_q, decode_q, page_owner, context_len)
    far = {0: message}
    for k in range(4, shards, 4):
        far[k] = swap(message, k)
    group = [0] + opening + second + third + near + last
    packed = pack(owners, page_counts, pages_k, pages_v, shards, capacity, group)
    for k, piece in zip(group, packed):
        pieces[k] = swap(piece, k) if k else piece
    own = jnp.concatenate([far[k] for k in range(0, shards, 4)], axis=0)
    across = swap(own, 2)
    beside = swap(own, 1)
    corner = swap(across, 1)
    keep, give, table = attend(
        rows_p,
        rows_d,
        capacity,
        page_counts,
        (own, beside, across, corner),
        cache_k,
        cache_v,
    )
    for bit in bits_of(shards):
        got = swap(give, bit)
        if 2 * bit < shards:
            keep, give = fold(rows, keep, got)
    parts = (keep, got)
    prefill_out, decode_out = merge(rows_p, rows_d, parts, message, decode_k, decode_v)
    stores = ()
    for group in ([0, first] + opening + second + near, third, last):
        stores = settle(shards, group, [pieces[k] for k in group], stores)
    store_page = table[:, :capacity].reshape(-1)
    return (
        prefill_out,
        decode_out.reshape(decode_q.shape),
        stores[0].reshape(-1, KVD),
        stores[1].reshape(-1, KVD),
        store_page,
    )


def solution(mesh):
    in_specs = (
        P(("groups", "seq"), None),
        P(("groups", "seq"), None),
        P(("groups", "seq"), None),
        P("groups"),
        P(("groups", "seq"), None),
        P(("groups", "seq"), None, None),
        P(("groups", "seq"), None, None),
        P(("groups", "seq"), None, None),
        P(("groups", "seq")),
    )
    out_specs = (
        P(("groups", "seq"), None),
        P(("groups", "seq"), None, None),
        P(("groups", "seq"), None),
        P(("groups", "seq"), None),
        P(("groups", "seq")),
    )
    return jax.shard_map(
        per_device, mesh=mesh, in_specs=in_specs, out_specs=out_specs, check_vma=False
    )
```

```python
import functools
import jax
import jax.numpy as jnp
from jax import lax
from jax.experimental import pallas as pl
from jax.experimental.pallas import tpu as pltpu
from jax.sharding import PartitionSpec as P

HQ = 64
KVH = 8
HD = 128
PAGE = 8
STEPS = 2
KVD = 1024
GRP = HQ // KVH
MASKED = -1e30
VMEM = pltpu.MemorySpace.VMEM
SMEM = pltpu.MemorySpace.SMEM
LIMIT = 32 * 1024 * 1024
SMALL = 8 * 1024 * 1024


def whole(space):
    return pl.BlockSpec(memory_space=space)


def message_kernel(rows_p, rows_d, length, prefill_q, decode_q, owners, out, rows):
    for r in range(rows_p + rows_d):
        ref, at = (prefill_q, r) if r < rows_p else (decode_q, r - rows_p)
        line = ref[at : at + 1, :].astype(jnp.float32)
        for h in range(HQ):
            rows[r * HQ + h : r * HQ + h + 1, :] = line[:, h * HD : (h + 1) * HD]
    base = (rows_p + rows_d) * HQ
    slots = owners.shape[1]
    rows[base : base + 8, :] = jnp.zeros((8, 128), jnp.float32)
    rows[base : base + 1, 0:slots] = owners[...].astype(jnp.float32)
    lane = lax.broadcasted_iota(jnp.int32, (1, 128), 1)
    digits = jnp.zeros((1, 128), jnp.int32)
    for q in range(length.shape[1]):
        value = length[:, q : q + 1]
        digits = jnp.where(lane == 2 * q, value >> 8, digits)
        digits = jnp.where(lane == 2 * q + 1, value & 255, digits)
    rows[base + 1 : base + 2, :] = digits.astype(jnp.float32)
    out[...] = rows[...].reshape(out.shape).astype(jnp.bfloat16)


def make_message(prefill_q, decode_q, page_owner, context_len):
    rows_p = prefill_q.shape[0]
    rows_d = decode_q.shape[0] * STEPS
    blocks = (rows_p + rows_d) * KVH + 1
    return pl.pallas_call(
        functools.partial(message_kernel, rows_p, rows_d),
        out_shape=jax.ShapeDtypeStruct((blocks, 8, 128), jnp.bfloat16),
        in_specs=[whole(VMEM)] * 4,
        out_specs=whole(VMEM),
        scratch_shapes=[pltpu.VMEM((blocks * 8, 128), jnp.float32)],
        name="message",
    )(context_len.reshape(1, -1), prefill_q, decode_q.reshape(rows_d, HQ * HD), page_owner.reshape(1, -1))


def pack_kernel(shards, capacity, partners, owners, counts, keys, values, *refs):
    outs, (taken, chosen) = refs[:-2], refs[-2:]
    me = lax.axis_index("seq")

    def reset(o, carry):
        taken[o] = 0
        return carry

    lax.fori_loop(0, shards, reset, 0, unroll=8)

    def note(j, carry):
        o = owners[j]
        k = taken[o]
        taken[o] = k + 1
        chosen[o * capacity + k] = j
        return carry

    lax.fori_loop(0, counts[me], note, 0)
    for partner, out in zip(partners, outs):
        o = me ^ partner
        count = taken[o]

        def copy(k, carry, o=o, count=count, out=out):
            full = k < count
            j = jnp.where(full, chosen[o * capacity + k], 0)
            for part, pages in enumerate((keys, values)):
                page = pages[j]
                out[part, k] = jnp.where(full, page, jnp.zeros_like(page))
            return carry

        lax.fori_loop(0, capacity, copy, 0, unroll=2)


def pack(owners, counts, keys, values, shards, capacity, partners):
    slots = keys.shape[0]
    piece = jax.ShapeDtypeStruct((2, capacity, PAGE, KVD), keys.dtype)
    return pl.pallas_call(
        functools.partial(pack_kernel, shards, capacity, partners),
        out_shape=(piece,) * len(partners),
        in_specs=[whole(SMEM), whole(SMEM), whole(VMEM), whole(VMEM)],
        out_specs=(whole(VMEM),) * len(partners),
        scratch_shapes=[
            pltpu.SMEM((shards,), jnp.int32),
            pltpu.SMEM((shards * capacity,), jnp.int32),
        ],
        cost_estimate=pl.CostEstimate(
            flops=0,
            transcendentals=0,
            bytes_accessed=(2 * slots + 4 * len(partners) * capacity) * PAGE * KVD * 2,
        ),
        name="pack",
    )(owners, counts, keys, values)


def pick_kernel(capacity, partner, owners, counts, keys, values, out, sem):
    me = lax.axis_index("seq")
    wanted = me ^ partner

    def fetch(j, k, start):
        for part, pages in enumerate((keys, values)):
            copy = pltpu.make_async_copy(pages.at[j], out.at[part, k], sem)
            if start:
                copy.start()
            else:
                copy.wait()

    def look(j, k):
        match = owners[j] == wanted

        @pl.when(match)
        def _():
            fetch(j, k, True)

        return k + match.astype(jnp.int32)

    found = lax.fori_loop(0, counts[me], look, jnp.int32(0))
    blank = jnp.zeros(out.shape[2:], out.dtype)

    def clear(k, carry):
        for part in range(2):
            out[part, k] = blank
        return carry

    lax.fori_loop(found, capacity, clear, 0)

    def arrive(k, carry):
        fetch(0, k, False)
        return carry

    lax.fori_loop(0, found, arrive, 0)


def pick(owners, counts, keys, values, capacity, partner):
    return pl.pallas_call(
        functools.partial(pick_kernel, capacity, partner),
        out_shape=jax.ShapeDtypeStruct((2, capacity, PAGE, KVD), keys.dtype),
        in_specs=[whole(SMEM), whole(SMEM), whole(pl.ANY), whole(pl.ANY)],
        out_specs=whole(VMEM),
        scratch_shapes=[pltpu.SemaphoreType.DMA],
        cost_estimate=pl.CostEstimate(
            flops=0, transcendentals=0, bytes_accessed=8 * capacity * PAGE * KVD
        ),
        name="pick",
    )(owners, counts, keys, values)


def attend_kernel(rows_p, rows_d, capacity, counts, *refs):
    messages, refs = refs[:4], refs[4:]
    keys, values, keep, give, table, limits, stats, hits = refs
    me = lax.axis_index("seq")
    rows = rows_p + rows_d
    blocks = rows * KVH + 1
    shards = 4 * messages[0].shape[0] // blocks
    height = shards * rows * GRP
    held = keys.shape[0]

    def block(k, at):
        return messages[k % 4][(k // 4) * blocks + at]

    def count(d, carry):
        before, total = carry
        here = counts[d]
        return (before + jnp.where(d < me, here, 0), total + here)

    before, total = lax.fori_loop(0, shards, count, (jnp.int32(0), jnp.int32(0)))
    start = PAGE * before
    live = PAGE * counts[me]
    first = PAGE * total - shards * rows_p + 1
    lane = lax.broadcasted_iota(jnp.int32, (1, 128), 1)
    for k in range(shards):
        d = me ^ k
        tail = block(k, rows * KVH).astype(jnp.float32)
        for r in range(rows):
            at = (k * rows + r) * GRP
            if r < rows_p:
                bound = jnp.minimum(first + d * rows_p + r - start, live)
                limits[at : at + GRP, :] = jnp.full((GRP, 128), bound, jnp.int32)
            else:
                q = (r - rows_p) // STEPS
                length = tail[1:2, 2 * q : 2 * q + 1] * 256.0 + tail[1:2, 2 * q + 1 : 2 * q + 2]
                bound = jnp.minimum(length.astype(jnp.int32) - start, live)
                limits[at : at + GRP, :] = jnp.broadcast_to(bound, (GRP, 128))
        hit = (tail[0:1, :].astype(jnp.int32) == me) & (lane < counts[d])
        hits[pl.ds(d, 1), :] = hit.astype(jnp.float32)

    hit = hits[...]
    earlier = (
        lax.broadcasted_iota(jnp.int32, (128, 128), 0)
        < lax.broadcasted_iota(jnp.int32, (128, 128), 1)
    ).astype(jnp.bfloat16)
    rank = jnp.dot(hit.astype(jnp.bfloat16), earlier, preferred_element_type=jnp.float32)
    wide = lax.broadcasted_iota(jnp.int32, hit.shape, 1)
    depth = lax.broadcasted_iota(jnp.int32, hit.shape, 0)
    numbered = jnp.zeros(hit.shape, jnp.float32)
    for k in range(capacity):
        match = jnp.where((hit > 0.5) & (rank == float(k)), (wide + 1).astype(jnp.float32), 0.0)
        found = jnp.sum(match, axis=1, keepdims=True)
        numbered = jnp.where(wide == k, found, numbered)
    within = numbered.astype(jnp.int32)
    slots = held // PAGE
    table[...] = jnp.where(within > 0, depth * slots + within - 1, -1)

    stats[...] = jnp.zeros_like(stats)
    spot = lax.broadcasted_iota(jnp.int32, (height, 128), 1)
    column = lax.broadcasted_iota(jnp.int32, (height, held), 1)
    pieces = [(k, r, (k * rows + r) * GRP) for k in range(shards) for r in range(rows)]

    def target(k):
        return give if k % 2 else keep

    def one_group(g, carry):
        query = jnp.concatenate(
            [block(k, r * KVH + g).astype(jnp.float32) for k, r, _ in pieces], axis=0
        ).astype(jnp.bfloat16)
        across = pl.ds(pl.multiple_of(g * HD, HD), HD)
        scores = lax.dot_general(
            query, keys[:, across], (((1,), (1,)), ((), ())), preferred_element_type=jnp.float32
        ) * (HD ** (-0.5))
        allowed = column < jnp.concatenate([limits[...]] * (held // 128), axis=1)
        scores = jnp.where(allowed, scores, MASKED)
        high = jnp.max(scores, axis=1, keepdims=True).astype(jnp.bfloat16).astype(jnp.float32)
        weights = jnp.where(allowed, jnp.exp(scores - high), 0.0)
        total = jnp.sum(weights, axis=1, keepdims=True)
        product = jnp.dot(
            weights.astype(jnp.bfloat16), values[:, across], preferred_element_type=jnp.float32
        )
        coarse = total.astype(jnp.bfloat16).astype(jnp.float32)
        kept = jnp.where(spot == g, high, stats[...])
        kept = jnp.where(spot == KVH + g, coarse, kept)
        stats[...] = jnp.where(spot == 2 * KVH + g, total - coarse, kept)
        for k, r, at in pieces:
            target(k)[k // 2, r * KVH + g] = product[at : at + GRP, :].astype(jnp.bfloat16)
        return carry

    lax.fori_loop(0, KVH, one_group, 0)
    for k, r, at in pieces:
        target(k)[k // 2, rows * KVH + r] = stats[at : at + GRP, :].astype(jnp.bfloat16)


def attend(rows_p, rows_d, capacity, counts, messages, keys, values):
    rows = rows_p + rows_d
    shards = 4 * messages[0].shape[0] // (rows * KVH + 1)
    height = shards * rows * GRP
    held = keys.shape[0]
    half = jax.ShapeDtypeStruct((shards // 2, rows * (KVH + 1), GRP, 128), jnp.bfloat16)
    return pl.pallas_call(
        functools.partial(attend_kernel, rows_p, rows_d, capacity),
        out_shape=(half, half, jax.ShapeDtypeStruct((shards, 128), jnp.int32)),
        in_specs=[whole(SMEM)] + [whole(VMEM)] * 6,
        out_specs=(whole(VMEM),) * 3,
        scratch_shapes=[
            pltpu.VMEM((height, 128), jnp.int32),
            pltpu.VMEM((height, 128), jnp.float32),
            pltpu.VMEM((shards, 128), jnp.float32),
        ],
        compiler_params=pltpu.CompilerParams(vmem_limit_bytes=LIMIT),
        cost_estimate=pl.CostEstimate(
            flops=4 * height * KVH * held * HD,
            transcendentals=height * KVH * held,
            bytes_accessed=2 * held * KVD * 2 + 4 * height * KVH * HD,
        ),
        name="attend",
    )(counts, *messages, keys, values)


def fold_kernel(rows, keep, got, *outs):
    lane = lax.broadcasted_iota(jnp.int32, (GRP, 128), 1)
    inside = lane < KVH

    def put(j, at, value):
        outs[j % 2][j // 2, at] = value.astype(jnp.bfloat16)

    for j in range(keep.shape[0]):
        for r in range(rows):
            raw = [ref[j, rows * KVH + r].astype(jnp.float32) for ref in (keep, got)]
            high = jnp.maximum(jnp.where(inside, raw[0], 0.0), jnp.where(inside, raw[1], 0.0))
            factors = [jnp.exp(jnp.where(inside, part, 0.0) - high) for part in raw]
            sizes = [
                pltpu.roll(part, 128 - KVH, 1) + pltpu.roll(part, 128 - 2 * KVH, 1) for part in raw
            ]
            total = jnp.where(inside, factors[0] * sizes[0] + factors[1] * sizes[1], 0.0)
            coarse = total.astype(jnp.bfloat16).astype(jnp.float32)
            line = high + pltpu.roll(coarse, KVH, 1) + pltpu.roll(total - coarse, 2 * KVH, 1)
            put(j, rows * KVH + r, line)
            for g in range(KVH):
                at = r * KVH + g
                mixed = factors[0][:, g : g + 1] * keep[j, at].astype(jnp.float32)
                mixed = mixed + factors[1][:, g : g + 1] * got[j, at].astype(jnp.float32)
                put(j, at, mixed)


def fold(rows, keep, got):
    half = jax.ShapeDtypeStruct((keep.shape[0] // 2,) + keep.shape[1:], keep.dtype)
    return pl.pallas_call(
        functools.partial(fold_kernel, rows),
        out_shape=(half, half),
        in_specs=[whole(VMEM)] * 2,
        out_specs=(whole(VMEM),) * 2,
        compiler_params=pltpu.CompilerParams(vmem_limit_bytes=LIMIT),
        cost_estimate=pl.CostEstimate(
            flops=keep.size * 4, transcendentals=0, bytes_accessed=keep.size * 6
        ),
        name="fold",
    )(keep, got)


def settle_kernel(partners, old, *refs):
    refs = refs[old:]
    pieces, (store_k, store_v, sems) = refs[: len(partners)], refs[len(partners) :]
    me = lax.axis_index("seq")
    puts = []
    for partner, piece in zip(partners, pieces):
        for part, store in enumerate((store_k, store_v)):
            puts.append(
                pltpu.make_async_copy(
                    piece.at[part], store.at[me ^ partner], sems.at[len(puts)]
                )
            )
    for put in puts:
        put.start()
    for put in puts:
        put.wait()


def settle(shards, partners, pieces, stores):
    number = len(partners)
    shape = (shards,) + pieces[0].shape[1:]
    store = jax.ShapeDtypeStruct(shape, pieces[0].dtype)
    return pl.pallas_call(
        functools.partial(settle_kernel, partners, len(stores)),
        out_shape=(store, store),
        in_specs=[whole(pl.ANY)] * len(stores) + [whole(VMEM)] * number,
        out_specs=(whole(pl.ANY),) * 2,
        input_output_aliases={i: i for i in range(len(stores))},
        scratch_shapes=[pltpu.SemaphoreType.DMA((2 * number,))],
        compiler_params=pltpu.CompilerParams(vmem_limit_bytes=SMALL),
        cost_estimate=pl.CostEstimate(
            flops=0, transcendentals=0, bytes_accessed=4 * number * pieces[0].size
        ),
        name="settle",
    )(*stores, *pieces)


def merge_kernel(rows_p, rows_d, message, new_k, new_v, *refs):
    parts, (prefill_out, decode_out, lines) = refs[:-3], refs[-3:]
    sources = len(parts)
    rows = rows_p + rows_d
    lane = lax.broadcasted_iota(jnp.int32, (GRP, 128), 1)
    for r in range(rows):
        raw = [part[0, rows * KVH + r].astype(jnp.float32) for part in parts]
        high = functools.reduce(jnp.maximum, raw)
        fresh = []
        if r >= rows_p:
            request, step = divmod(r - rows_p, STEPS)
            for t in range(step + 1):
                score = jnp.zeros((GRP, 128), jnp.float32)
                for g in range(KVH):
                    query = message[r * KVH + g].astype(jnp.float32)
                    at = request * STEPS + t
                    key = new_k[at : at + 1, g * HD : (g + 1) * HD].astype(jnp.float32)
                    column = jnp.sum(query * key, axis=1, keepdims=True) * (HD ** (-0.5))
                    score = jnp.where(lane == g, column, score)
                fresh.append((request * STEPS + t, score))
                high = jnp.maximum(high, score)
        high = jnp.where(lane < KVH, high, 0.0)
        total = jnp.zeros((GRP, 128), jnp.float32)
        factors = []
        for s in range(sources):
            factor = jnp.exp(jnp.where(lane < KVH, raw[s], 0.0) - high)
            size = pltpu.roll(raw[s], 128 - KVH, 1) + pltpu.roll(raw[s], 128 - 2 * KVH, 1)
            total = total + factor * size
            factors.append(factor)
        fresh = [(at, jnp.exp(score - high)) for at, score in fresh]
        for _, weight in fresh:
            total = total + weight
        total = jnp.where(lane < KVH, total, 1.0)
        factors = [factor / total for factor in factors]
        fresh = [
            (at, (weight / total).astype(jnp.bfloat16).astype(jnp.float32)) for at, weight in fresh
        ]
        for g in range(KVH):
            result = jnp.zeros((GRP, HD), jnp.float32)
            for s in range(sources):
                block = parts[s][0, r * KVH + g].astype(jnp.float32)
                result = result + factors[s][:, g : g + 1] * block
            for at, weight in fresh:
                value = new_v[at : at + 1, g * HD : (g + 1) * HD].astype(jnp.float32)
                result = result + weight[:, g : g + 1] * value
            for h in range(GRP):
                column = (g * GRP + h) * HD
                lines[r : r + 1, column : column + HD] = result[h : h + 1, :]
    prefill_out[...] = lines[0:rows_p, :].astype(jnp.bfloat16)
    decode_out[...] = lines[rows_p:rows, :].astype(jnp.bfloat16)


def merge(rows_p, rows_d, parts, message, new_k, new_v):
    rows = rows_p + rows_d
    return pl.pallas_call(
        functools.partial(merge_kernel, rows_p, rows_d),
        out_shape=(
            jax.ShapeDtypeStruct((rows_p, HQ * HD), jnp.bfloat16),
            jax.ShapeDtypeStruct((rows_d, HQ * HD), jnp.bfloat16),
        ),
        in_specs=[whole(VMEM)] * (3 + len(parts)),
        out_specs=(whole(VMEM), whole(VMEM)),
        scratch_shapes=[pltpu.VMEM((rows, HQ * HD), jnp.float32)],
        compiler_params=pltpu.CompilerParams(vmem_limit_bytes=LIMIT),
        cost_estimate=pl.CostEstimate(
            flops=len(parts) * parts[0].size * 4,
            transcendentals=0,
            bytes_accessed=len(parts) * parts[0].size * 2,
        ),
        name="merge",
    )(message, new_k.reshape(rows_d, KVD), new_v.reshape(rows_d, KVD), *parts)


def swap(array, distance):
    shards = lax.axis_size("seq")
    return lax.ppermute(array, "seq", [(i, i ^ distance) for i in range(shards)])


def send_order(shards):
    upper = range(shards // 2, shards)
    side = range(4, shards // 2)
    plain, plain_side = [[k for k in group if not k & 2] for group in (upper, side)]
    other, other_side = [[k for k in group if k & 2] for group in (upper, side)]
    half = len(other) // 2
    other = other[half:] + other[:half]
    first = plain[0]
    opening = plain_side[: len(plain_side) // 2] + plain[1:2]
    second = plain_side[len(plain_side) // 2 :] + plain[2:]
    third = other[:half] + other_side
    return first, opening, second, third, [1, 2, 3], other[half:]


def bits_of(shards):
    return [1 << b for b in range(shards.bit_length() - 1)]


def per_device(
    prefill_q, cache_k, cache_v, page_counts, page_owner, decode_q, decode_k, decode_v, context_len
):
    shards = lax.axis_size("seq")
    page_slots = cache_k.shape[0] // PAGE
    capacity = max(2, 2 * page_slots // shards)
    rows_p = prefill_q.shape[0]
    rows_d = decode_q.shape[0] * STEPS
    owners = page_owner.reshape(-1)
    pages_k = cache_k.reshape(page_slots, PAGE, KVD)
    pages_v = cache_v.reshape(page_slots, PAGE, KVD)
    rows = rows_p + rows_d
    first, opening, second, third, near, last = send_order(shards)
    piece = pick(owners, page_counts, pages_k, pages_v, capacity, first)
    pieces = {first: swap(piece, first)}
    message = make_message(prefill_q, decode_q, page_owner, context_len)
    far = {0: message}
    for bit in reversed(bits_of(shards)[2:]):
        for k in list(far):
            far[k | bit] = swap(far[k], bit)
    group = [0] + opening + second + third + near + last
    packed = pack(owners, page_counts, pages_k, pages_v, shards, capacity, group)
    for k, piece in zip(group, packed):
        pieces[k] = swap(piece, k) if k else piece
    own = jnp.concatenate([far[k] for k in range(0, shards, 4)], axis=0)
    across = swap(own, 2)
    beside = swap(own, 1)
    corner = swap(across, 1)
    keep, give, table = attend(
        rows_p,
        rows_d,
        capacity,
        page_counts,
        (own, beside, across, corner),
        cache_k,
        cache_v,
    )
    for bit in bits_of(shards):
        got = swap(give, bit)
        if 2 * bit < shards:
            keep, give = fold(rows, keep, got)
    parts = (keep, got)
    prefill_out, decode_out = merge(rows_p, rows_d, parts, message, decode_k, decode_v)
    stores = ()
    for group in ([0, first] + opening + second + near, third, last):
        stores = settle(shards, group, [pieces[k] for k in group], stores)
    store_page = table[:, :capacity].reshape(-1)
    return (
        prefill_out,
        decode_out.reshape(decode_q.shape),
        stores[0].reshape(-1, KVD),
        stores[1].reshape(-1, KVD),
        store_page,
    )


def solution(mesh):
    in_specs = (
        P(("groups", "seq"), None),
        P(("groups", "seq"), None),
        P(("groups", "seq"), None),
        P("groups"),
        P(("groups", "seq"), None),
        P(("groups", "seq"), None, None),
        P(("groups", "seq"), None, None),
        P(("groups", "seq"), None, None),
        P(("groups", "seq")),
    )
    out_specs = (
        P(("groups", "seq"), None),
        P(("groups", "seq"), None, None),
        P(("groups", "seq"), None),
        P(("groups", "seq"), None),
        P(("groups", "seq")),
    )
    return jax.shard_map(
        per_device, mesh=mesh, in_specs=in_specs, out_specs=out_specs, check_vma=False
    )
```
